512 devices in a mesh: inst: 64 (over z_hi, x, y), tp: 8 (over z_lo, core).
Axes of the slice: x: 4, y: 8, z: 8 (z_hi: 2, z_lo: 4; z = z_hi * 4 + z_lo), core: 2. Of those that a mesh axis runs over, the one named last changes fastest.
Arguments:
- step_queries: bfloat16 [4, 512, 8192], P(None, 'inst', 'tp'), may hold values from -11 to 11
- step_keyvals: bfloat16 [4, 512, 8, 256], P(None, 'inst', 'tp'), may hold values from -9.5 to 9.5
- cache_pages: bfloat16 [8192, 16, 8, 256], P('inst', None, 'tp'), may hold values from -9.5 to 9.5
- block_table: int32 [512, 16], P('inst'), may hold values from 0 to 127, as said below
- context_len: int32 [512], replicated, may hold values from 1 to 256, as said below
- partner: int32 [64], replicated, may hold values from 0 to 63, as said below
- moved_slot: int32 [64], replicated, may hold values from 0 to 7
- prompt_queries: bfloat16 [32768, 8192], P(('inst', 'tp')), may hold values from -11 to 11
- prompt_keyvals: bfloat16 [32768, 8, 256], P(('inst', 'tp')), may hold values from -9.5 to 9.5
- prompt_target: int32 [32768, 1], replicated, may hold values from 0 to 63; in each aligned block of 64 rows (0 to 63, 64 to 127, ...) at most 2 rows name the same one
Outputs:
- decode_output: bfloat16 [4, 512, 8192], P(None, 'inst', 'tp')
- prefill_output: bfloat16 [65536, 8192], P('inst', 'tp')
The draws below stay inside these ranges and needn't reach their ends.
Inputs may be any that keep to these rules, and one draw needn't show every extreme that they name: partner[partner[i]] = i, and i and partner[i] differ in exactly one bit. `block_table`: the 8 rows of one instance together name each of its 128 pages once. `context_len`: some request holds exactly 256 tokens. `prompt_target`: among the 64 rows of one device no instance is named more than 2 times.
All inputs are finite; a program needn't handle non-finite values.
Results may differ from the reference program's by a relative error of at most 0.0049.
Values may be sent and summed in bfloat16 or wider, within the bound.
No kernel may reach another device: no remote copies, remote signals or barrier semaphores. Data moves between devices by JAX's collectives and lax.ppermute only.
A program may use at most 64 MiB of HBM per device.

```python
import math
import jax
import jax.numpy as jnp
import numpy as np
from jax import lax

H = 64
KVH = 8
HD = 128
REQ = 8
PAGE = 16
MAXP = 16
STEPS = 4
ROWS_DEV = 64
CTX = 256
POOL = 128
CAP = 2
SLOTS = 1024
ROWS = 32768
N_INST = 64
N_TP = 8


def keyval_law(key, shape):
    drawn = jnp.clip(jax.random.normal(key, shape, jnp.float32), -6.0, 6.0)
    return drawn.astype(jnp.bfloat16)


def query_law(key, shape):
    drawn = jnp.clip(jax.random.normal(key, shape, jnp.float32), -6.0, 6.0)
    return drawn.astype(jnp.bfloat16)


def draw_step_queries(key, part):
    return query_law(jax.random.fold_in(key, 21), (STEPS, N_INST * REQ, H * HD))


def draw_step_keyvals(key, part):
    return keyval_law(jax.random.fold_in(key, 22), (STEPS, N_INST * REQ, KVH, 2 * HD))


def draw_cache_pages(key, part):
    return keyval_law(jax.random.fold_in(key, 23), (N_INST * POOL, PAGE, KVH, 2 * HD))


def draw_prompt_queries(key, part):
    return query_law(jax.random.fold_in(key, 24), (ROWS, H * HD))


def draw_prompt_keyvals(key, part):
    return keyval_law(jax.random.fold_in(key, 25), (ROWS, KVH, 2 * HD))


def shuffled_pool(key):
    return jax.random.permutation(key, POOL).astype(jnp.int32)


def draw_block_table(key, part):
    keys = jax.random.split(jax.random.fold_in(key, 31), N_INST)
    tables = jax.vmap(shuffled_pool)(keys)
    return tables.reshape(N_INST * REQ, MAXP).astype(jnp.int32)


def draw_context_len(key, part):
    base = jax.random.fold_in(key, 41)
    lengths = jax.random.randint(base, (N_INST * REQ,), 1, CTX + 1, dtype=jnp.int32)
    spot = jax.random.randint(jax.random.fold_in(base, 1), (), 0, N_INST * REQ, dtype=jnp.int32)
    return lengths.at[spot].set(CTX).astype(jnp.int32)


def draw_partner(key, part):
    base = jax.random.fold_in(key, 51)
    width = N_INST.bit_length() - 1
    index = jnp.arange(N_INST, dtype=jnp.int32)
    order = jax.random.permutation(jax.random.fold_in(base, 1), width).astype(jnp.int32)
    flags = jax.random.randint(jax.random.fold_in(base, 2), (width, N_INST), 0, 2, dtype=jnp.int32)
    chosen = jnp.full((N_INST,), -1, dtype=jnp.int32)
    for level in range(width):
        cube = jnp.zeros((N_INST,), dtype=jnp.int32)
        for lower in range(level):
            digit = jnp.bitwise_and(jnp.right_shift(index, order[lower]), 1)
            cube = cube + jnp.left_shift(digit, lower)
        flag = flags[level][cube]
        if level == width - 1:
            flag = jnp.ones_like(flag)
        chosen = jnp.where((chosen < 0) & (flag > 0), order[level], chosen)
    return jnp.bitwise_xor(index, jnp.left_shift(jnp.int32(1), chosen)).astype(jnp.int32)


def place_ends(drawn, stream_key, smallest, high):
    index_at = [jax.random.randint(jax.random.fold_in(stream_key, axis), (), 0, length) for axis, length in enumerate(drawn.shape)]
    longest = drawn.shape.index(max(drawn.shape))
    neighbour = index_at[:longest] + [(index_at[longest] + 1) % drawn.shape[longest]] + index_at[longest + 1:]
    return drawn.at[tuple(index_at)].set(smallest).at[tuple(neighbour)].set(high)


def deal_out(own_key, own, number, rows, number_of, top, bound, lean):
    order = jax.random.permutation(own_key, number_of)
    packed, ordinary = load_shares(number_of, rows * top, bound, lean, True), load_shares(number_of, rows * top, bound, lean, False)
    places = jnp.arange(number_of)

    def named(sizes, rotation):
        used = int((sizes > 0).sum())
        fixed = max(1, used // 4)
        moved = fixed + (places - fixed + rotation * (used - fixed)) % max(1, number_of - fixed)
        return jnp.zeros((number_of,), jnp.int32).at[order[jnp.where(places < fixed, places, moved)]].set(jnp.asarray(sizes, jnp.int32))

    sizes = jnp.where(number % 4 == 0, named(packed, number // 4), named(ordinary, number - number // 4 - 1))
    mixed = jax.random.permutation(jax.random.fold_in(own, 3), number_of)
    source_of, receiver = mixed[0:number_of // 2 * 2:2], mixed[1:number_of // 2 * 2:2]
    margin = jnp.minimum(sizes[source_of] - 1, bound - sizes[receiver]) // 2
    margin = jnp.where((source_of == order[0]) | (receiver == order[0]) | (sizes[receiver] == 0), 0, jnp.maximum(margin, 0))
    moved = jax.random.randint(jax.random.fold_in(own, 4), (number_of // 2,), 0, 1 << 20) % (margin + 1)
    sizes = sizes.at[source_of].add(-moved).at[receiver].add(moved)
    members = jnp.searchsorted(jnp.cumsum(sizes), jnp.arange(rows * top), side="right").astype(jnp.int32)
    listing = members.reshape(top, rows).T
    listing = listing[jax.random.permutation(jax.random.fold_in(own, 1), rows)]
    rotation = jax.random.randint(jax.random.fold_in(own, 2), (rows, 1), 0, top)
    return jnp.take_along_axis(listing, (jnp.arange(top)[None, :] + rotation) % top, axis=1)


def load_shares(number_of, total, most, slope, full):
    loads = [(1 << 20) // math.isqrt(standing ** slope) + 1 for standing in range(1, number_of + 1)]
    largest = most if full else min(most, max(-(-total // number_of), total * loads[0] // sum(loads)))
    least = 1 if total - largest >= number_of - 1 else 0
    given, rest = [largest] + [least] * (number_of - 1), total - largest - least * (number_of - 1)
    while rest > 0:
        movable = [i for i in range(1, number_of) if given[i] < largest] or [i for i in range(1, number_of) if given[i] < most]
        pool, budget = sum([loads[i] for i in movable]), rest
        for i in movable:
            extra = min(most - given[i], max(1, budget * loads[i] // pool), rest)
            given[i] = given[i] + extra
            rest = rest - extra
    return np.array(given)


def setup_inputs(seed: int = 0) -> dict:
    seeds = jax.random.split(jax.random.key(seed), 11)
    step_queries = draw_step_queries(jax.random.fold_in(seeds[10], 71), 0)
    step_keyvals = draw_step_keyvals(jax.random.fold_in(seeds[10], 71), 0)
    cache_pages = draw_cache_pages(jax.random.fold_in(seeds[10], 71), 0)
    block_table = draw_block_table(jax.random.fold_in(seeds[10], 71), 0)
    context_len = draw_context_len(jax.random.fold_in(seeds[10], 71), 0)
    partner = draw_partner(jax.random.fold_in(seeds[10], 71), 0)
    moved_slot = place_ends(jax.random.randint(seeds[6], (N_INST,), 0, REQ), jax.random.fold_in(seeds[6], 1), 0, REQ - 1).astype(jnp.int32)
    prompt_queries = draw_prompt_queries(jax.random.fold_in(seeds[10], 71), 0)
    prompt_keyvals = draw_prompt_keyvals(jax.random.fold_in(seeds[10], 71), 0)
    prompt_target_keys = jax.random.split(jax.random.fold_in(seeds[9], 1), ROWS // ROWS_DEV)
    prompt_target_turns = jax.random.permutation(jax.random.fold_in(seeds[9], 3), ROWS // ROWS_DEV)
    prompt_target = jax.vmap(lambda own, number: deal_out(jax.random.fold_in(seeds[9], 2), own, number, ROWS_DEV, N_INST, 1, CAP, 2))(prompt_target_keys, prompt_target_turns).reshape((ROWS, 1))
    return {"step_queries": step_queries, "step_keyvals": step_keyvals, "cache_pages": cache_pages, "block_table": block_table, "context_len": context_len, "partner": partner, "moved_slot": moved_slot, "prompt_queries": prompt_queries, "prompt_keyvals": prompt_keyvals, "prompt_target": prompt_target}


def masked_weights(scores, mask):
    shifted = jnp.where(mask, scores, jnp.float32(-1e30))
    top = jnp.max(shifted, axis=-1, keepdims=True)
    expo = jnp.where(mask, jnp.exp(shifted - top), jnp.float32(0.0))
    total = jnp.sum(expo, axis=-1, keepdims=True)
    total = jnp.where(total > 0, total, jnp.float32(1.0))
    return expo / total


def round_weights(weights):
    rounded = lax.optimization_barrier(weights.astype(jnp.bfloat16))
    return rounded.astype(jnp.float32)


def decode_part(step_queries, step_keyvals, cache_pages, block_table, context_len, partner, moved_slot):
    group = H // KVH
    scale = HD ** -0.5
    inst = jnp.arange(N_INST, dtype=jnp.int32)
    slot = jnp.arange(REQ, dtype=jnp.int32)
    moved = slot[None, :] == moved_slot[:, None]
    src_inst = jnp.where(moved, partner[:, None], inst[:, None]).astype(jnp.int32)
    src_slot = jnp.where(moved, moved_slot[partner][:, None], slot[None, :]).astype(jnp.int32)
    source = (src_inst * REQ + src_slot).reshape(-1).astype(jnp.int32)
    pages = (block_table[source] + (src_inst.reshape(-1) * POOL)[:, None]).astype(jnp.int32)
    lengths = context_len[source]

    def one_request(items):
        queries, fresh, page_ids, length = items
        context = cache_pages[page_ids].reshape(CTX, KVH, 2 * HD).astype(jnp.float32)
        fresh = fresh.astype(jnp.float32)
        query = queries.astype(jnp.float32).reshape(STEPS, KVH, group, HD)
        past = jnp.einsum('tkgd,ckd->tkgc', query, context[:, :, :HD]) * scale
        newer = jnp.einsum('tkgd,ukd->tkgu', query, fresh[:, :, :HD]) * scale
        past_mask = jnp.broadcast_to((jnp.arange(CTX, dtype=jnp.int32) < length)[None, None, None, :], past.shape)
        step_ids = jnp.arange(STEPS, dtype=jnp.int32)
        new_mask = jnp.broadcast_to((step_ids[None, :] <= step_ids[:, None])[:, None, None, :], newer.shape)
        weights = masked_weights(jnp.concatenate([past, newer], axis=-1), jnp.concatenate([past_mask, new_mask], axis=-1))
        weights = round_weights(weights)
        out = jnp.einsum('tkgc,ckd->tkgd', weights[..., :CTX], context[:, :, HD:])
        out = out + jnp.einsum('tkgu,ukd->tkgd', weights[..., CTX:], fresh[:, :, HD:])
        return out.reshape(STEPS, H * HD).astype(jnp.bfloat16)

    decoded = lax.map(one_request, (jnp.transpose(step_queries, (1, 0, 2)), jnp.transpose(step_keyvals, (1, 0, 2, 3)), pages, lengths))
    return jnp.transpose(decoded, (1, 0, 2))


def prefill_part(prompt_queries, prompt_keyvals, prompt_target):
    group = H // KVH
    scale = HD ** -0.5
    devices = N_INST * N_TP
    target = prompt_target[:, 0].reshape(devices, ROWS_DEV).astype(jnp.int32)
    onehot = (target[:, :, None] == jnp.arange(N_INST, dtype=jnp.int32)[None, None, :]).astype(jnp.int32)
    before = (jnp.cumsum(onehot, axis=1) - onehot).astype(jnp.int32)
    rank = jnp.sum(before * onehot, axis=2).astype(jnp.int32)
    slot = (jnp.arange(devices, dtype=jnp.int32)[:, None] * CAP + rank).astype(jnp.int32)
    table = jnp.full((N_INST, SLOTS), -1, dtype=jnp.int32)
    table = table.at[target.reshape(-1), slot.reshape(-1)].set(jnp.arange(ROWS, dtype=jnp.int32))
    positions = jnp.arange(SLOTS, dtype=jnp.int32)

    def one_instance(row_ids):
        valid = row_ids >= 0
        safe = jnp.maximum(row_ids, 0).astype(jnp.int32)
        query = prompt_queries[safe].astype(jnp.float32).reshape(SLOTS, KVH, group, HD)
        keyval = prompt_keyvals[safe].astype(jnp.float32)
        mask = (valid[None, :] & (positions[None, :] <= positions[:, None]))[None]

        def one_head(items):
            head_query, head_keyval = items
            scores = jnp.einsum('qgd,cd->gqc', head_query, head_keyval[:, :HD]) * scale
            weights = round_weights(masked_weights(scores, jnp.broadcast_to(mask, scores.shape)))
            return jnp.einsum('gqc,cd->qgd', weights, head_keyval[:, HD:])

        outs = lax.map(one_head, (jnp.transpose(query, (1, 0, 2, 3)), jnp.transpose(keyval, (1, 0, 2))))
        outs = jnp.transpose(outs, (1, 0, 2, 3)).reshape(SLOTS, H * HD)
        return jnp.where(valid[:, None], outs, jnp.float32(0.0)).astype(jnp.bfloat16)

    return lax.map(one_instance, table).reshape(N_INST * SLOTS, H * HD)


def reference(step_queries, step_keyvals, cache_pages, block_table, context_len, partner, moved_slot, prompt_queries, prompt_keyvals, prompt_target):
    decode_output = decode_part(step_queries, step_keyvals, cache_pages, block_table, context_len, partner, moved_slot)
    prefill_output = prefill_part(prompt_queries, prompt_keyvals, prompt_target)
    return (decode_output, prefill_output)
```

```python
import functools
import math

import jax
import jax.numpy as jnp
from jax import lax
from jax.experimental import pallas as pl
from jax.experimental.pallas import tpu as pltpu
from jax.sharding import PartitionSpec as P

H, KVH, HD = 64, 8, 128
REQ, PAGE, MAXP, STEPS = 8, 16, 16, 4
ROWS_DEV, CTX, POOL, CAP, SLOTS = 64, 256, 128, 2, 1024
N_INST, N_TP = 64, 8
GROUP = H // KVH
TILES = GROUP + 2
MESSAGE = TILES * CAP
LANES = 128
LOG2_SCALE = HD**-0.5 * math.log2(math.e)
MASKED = -1e30
VMEM = 48 * 1024 * 1024


def iota(shape, dim):
    return lax.broadcasted_iota(jnp.int32, shape, dim)


def dot(a, b, contract=((1,), (0,))):
    return lax.dot_general(a, b, (contract, ((), ())), preferred_element_type=jnp.float32)


NT = ((1,), (1,))


INSTS = 8


def dispatch_kernel(me_ref, target_ref, queries_ref, keyvals_ref, out_ref, place_ref, rows_ref):
    step = pl.program_id(0)

    @pl.when(step == 0)
    def _():
        me = me_ref[0]
        line = lax.rem(lax.div(me, 2), 8)
        both = jnp.sum(
            jnp.where(iota((8, LANES), 0) == line, target_ref[...], 0), axis=0, keepdims=True
        )
        both = jnp.broadcast_to(both, (8, LANES))
        other = pltpu.roll(both, ROWS_DEV, 1)
        first = iota((8, LANES), 1) < ROWS_DEV
        odd = lax.rem(me, 2) == 1
        mine = jnp.where(first != odd, both, other)[0:1]
        down, along = iota((ROWS_DEV, LANES), 0), iota((ROWS_DEV, LANES), 1)
        wide = jnp.broadcast_to(mine, (ROWS_DEV, LANES))
        column = jnp.sum(jnp.where(down == along, wide, 0), axis=1, keepdims=True)
        earlier = (column == wide) & (down < along % ROWS_DEV)
        rank = jnp.sum(earlier.astype(jnp.int32), axis=0, keepdims=True)
        place = jnp.broadcast_to(mine * CAP + rank, (8, LANES))
        for i in range(4):
            place_ref[:, i * LANES : (i + 1) * LANES] = place
        down, along = iota((512, 512), 0), iota((512, 512), 1)
        order = (down % ROWS_DEV == along // KVH) & (down // ROWS_DEV == along % KVH)
        keyvals = dot(order.astype(jnp.float32).astype(jnp.bfloat16), keyvals_ref[...])
        keyvals = keyvals.astype(jnp.bfloat16)
        for c in range(N_TP * TILES):
            tp, tile = divmod(c, TILES)
            if tile < GROUP:
                piece = queries_ref[:, (tp * GROUP + tile) * HD : (tp * GROUP + tile + 1) * HD]
            else:
                lane = (tile - GROUP) * HD
                piece = keyvals[tp * ROWS_DEV : (tp + 1) * ROWS_DEV, lane : lane + HD]
            to, col = c % 8, c // 8
            rows_ref[to * ROWS_DEV : (to + 1) * ROWS_DEV, col * LANES : (col + 1) * LANES] = piece

    down, along = iota((LANES, 512), 0), iota((LANES, 512), 1)
    wanted = (step * INSTS + down // 16) * CAP + down % 2
    place = jnp.broadcast_to(place_ref[0:1, :], (LANES, 512))
    chosen = (place == wanted) & (along // ROWS_DEV == down // 2 % 8)
    out = dot(chosen.astype(jnp.float32).astype(jnp.bfloat16), rows_ref[...])
    out = out.astype(jnp.bfloat16)
    for i in range(INSTS):
        for col in range(TILES):
            out_ref[i * 160 + col * 16 : i * 160 + (col + 1) * 16, :] = out[
                i * 16 : (i + 1) * 16, col * LANES : (col + 1) * LANES
            ]


def dispatch(me, targets, queries, keyvals):
    rows = N_INST * N_TP * MESSAGE
    return pl.pallas_call(
        dispatch_kernel,
        out_shape=jax.ShapeDtypeStruct((rows, LANES), jnp.bfloat16),
        grid_spec=pltpu.PrefetchScalarGridSpec(
            num_scalar_prefetch=1,
            grid=(N_INST // INSTS,),
            in_specs=[
                pl.BlockSpec((8, LANES), lambda s, me: (me[0] // 16, 0)),
                pl.BlockSpec((ROWS_DEV, H * HD), lambda s, me: (0, 0)),
                pl.BlockSpec((ROWS_DEV * KVH, 2 * HD), lambda s, me: (0, 0)),
            ],
            out_specs=pl.BlockSpec((rows * INSTS // N_INST, LANES), lambda s, me: (s, 0)),
            scratch_shapes=[
                pltpu.VMEM((8, 512), jnp.int32),
                pltpu.VMEM((512, TILES * LANES), jnp.bfloat16),
            ],
        ),
        compiler_params=pltpu.CompilerParams(vmem_limit_bytes=VMEM),
        name="dispatch",
    )(me, targets, queries, keyvals)


def decode_kernel(
    info_ref, lens_ref, table_ref, queries_ref, fresh_ref, came_ref, cache_ref, target_ref,
    out_ref, bias_ref, valid_ref,
):
    inst, moved = info_ref[0], info_ref[1]
    rows = STEPS * REQ
    traded = iota((rows, 1), 0) % REQ == moved

    def merged(own, lanes):
        came = came_ref[:, lanes].astype(jnp.float32)
        came = jnp.broadcast_to(came[:, None, :], (STEPS, REQ, came.shape[1]))
        came = came.reshape(rows, came.shape[2])
        return jnp.where(traded, came, own.astype(jnp.float32)).astype(jnp.bfloat16)

    queries = merged(queries_ref[...], slice(0, GROUP * HD))
    fresh = merged(fresh_ref[...], slice(GROUP * HD, (GROUP + 2) * HD))
    query = jnp.concatenate([queries[:, g * HD : (g + 1) * HD] for g in range(GROUP)], axis=0)
    n = GROUP * rows
    row = iota((n, 1), 0)
    request, moment = row % REQ, row // REQ % STEPS
    newer = dot(query, fresh[:, :HD], NT)
    along = iota((n, rows), 1)
    newer = jnp.where((along % REQ == request) & (along // REQ <= moment), newer, MASKED)
    past = jnp.zeros((n, CTX), jnp.float32)
    length = jnp.zeros((n, 1), jnp.int32)
    values = []
    for r in range(REQ):
        pages = [
            cache_ref[pl.ds(pl.multiple_of(table_ref[r, j] * PAGE, PAGE), PAGE), :]
            for j in range(MAXP)
        ]
        context = jnp.concatenate(pages, axis=0)
        values.append(context[:, HD:])
        past = jnp.where(request == r, dot(query, context[:, :HD], NT), past)
        length = jnp.where(request == r, lens_ref[inst * REQ + r], length)
    past = jnp.where(iota((n, CTX), 1) < length, past, MASKED)
    top = jnp.maximum(
        jnp.max(past, axis=1, keepdims=True), jnp.max(newer, axis=1, keepdims=True)
    )
    past = jnp.exp2((past - top) * LOG2_SCALE)
    newer = jnp.exp2((newer - top) * LOG2_SCALE)
    total = jnp.sum(past, axis=1, keepdims=True) + jnp.sum(newer, axis=1, keepdims=True)
    past, newer = past / total, newer / total
    out = dot(newer.astype(jnp.bfloat16), fresh[:, HD:])
    for r in range(REQ):
        weights = jnp.where(request == r, past, 0.0).astype(jnp.bfloat16)
        out = out + dot(weights, values[r])
    for g in range(GROUP):
        out_ref[:, g * HD : (g + 1) * HD] = out[g * rows : (g + 1) * rows].astype(jnp.bfloat16)

    lines = target_ref.shape[0]
    hits = (target_ref[...] == inst).astype(jnp.float32).astype(jnp.bfloat16)
    slot, along = iota((SLOTS, lines), 0), iota((SLOTS, lines), 1)
    spread = dot((slot // 4 == along).astype(jnp.float32).astype(jnp.bfloat16), hits)
    slot, along = iota((SLOTS, LANES), 0), iota((SLOTS, LANES), 1)
    spread = jnp.where(along // ROWS_DEV == slot // 2 % 2, spread, 0.0).astype(jnp.bfloat16)
    count = dot(spread, jnp.ones((LANES, LANES), jnp.bfloat16))
    valid_ref[...] = (count > (slot % 2).astype(jnp.float32)).astype(jnp.float32)
    count = dot(jnp.ones((8, LANES), jnp.bfloat16), spread, NT)
    rank = (iota((8, SLOTS), 1) % 2).astype(jnp.float32)
    bias_ref[...] = jnp.where(count > rank, 0.0, MASKED)


def decode(info, lens, table, queries, fresh, came, cache, targets):
    smem, vmem = (pl.BlockSpec(memory_space=s) for s in (pltpu.SMEM, pltpu.VMEM))
    return pl.pallas_call(
        decode_kernel,
        out_shape=(
            jax.ShapeDtypeStruct(queries.shape, jnp.bfloat16),
            jax.ShapeDtypeStruct((8, SLOTS), jnp.float32),
            jax.ShapeDtypeStruct((SLOTS, LANES), jnp.float32),
        ),
        in_specs=[smem, smem, smem, vmem, vmem, vmem, vmem, vmem],
        out_specs=(vmem, vmem, vmem),
        compiler_params=pltpu.CompilerParams(vmem_limit_bytes=VMEM),
        name="decode",
    )(info, lens, table, queries, fresh, came, cache, targets)


BLOCK = 256


def prefill_kernel(arrived_ref, bias_ref, valid_ref, out_ref, packed_ref, causal_ref):
    step = pl.program_id(0)

    @pl.when(step == 0)
    def _():
        size = N_TP * MESSAGE
        to, src = iota((size, size), 0), iota((size, size), 1)
        order = (
            (to // 16 == src // 2 % TILES) & (to // 2 % 8 == src // MESSAGE) & (to % 2 == src % 2)
        )
        order = order.astype(jnp.float32).astype(jnp.bfloat16)
        for i in range(0, N_INST, 8):
            rows = jnp.concatenate(
                [arrived_ref[(i + j) * size : (i + j + 1) * size, :] for j in range(8)], axis=1
            )
            rows = dot(order, rows).astype(jnp.bfloat16)
            for tile in range(TILES):
                for j in range(8):
                    packed_ref[tile, (i + j) * 16 : (i + j + 1) * 16, :] = rows[
                        tile * 16 : (tile + 1) * 16, j * LANES : (j + 1) * LANES
                    ]
        causal_ref[...] = jnp.where(
            iota((BLOCK, BLOCK), 1) <= iota((BLOCK, BLOCK), 0), 0.0, MASKED
        )

    def block(start):
        end = start + BLOCK
        keys, values = packed_ref[GROUP, :end, :], packed_ref[GROUP + 1, :end, :]
        bias = bias_ref[0:1, :end]
        own = causal_ref[...] + bias[:, start:]
        filled = valid_ref[start:end, 0:1]
        for h in range(GROUP):
            scores = dot(packed_ref[h, start:end, :], keys, NT)
            last = scores[:, start:] + own
            top = jnp.max(last, axis=1, keepdims=True)
            if start:
                scores = scores[:, :start] + bias[:, :start]
                top = jnp.maximum(top, jnp.max(scores, axis=1, keepdims=True))
                scores = jnp.concatenate([scores, last], axis=1)
            else:
                scores = last
            expo = jnp.exp2((scores - top) * LOG2_SCALE)
            share = filled / jnp.sum(expo, axis=1, keepdims=True)
            out = dot((expo * share).astype(jnp.bfloat16), values)
            out_ref[:, h * HD : (h + 1) * HD] = out.astype(jnp.bfloat16)

    for i in range(SLOTS // BLOCK):
        pl.when(step == i)(functools.partial(block, i * BLOCK))


def prefill(arrived, bias, valid):
    whole = lambda s: (0, 0)
    return pl.pallas_call(
        prefill_kernel,
        out_shape=jax.ShapeDtypeStruct((SLOTS, GROUP * HD), jnp.bfloat16),
        grid=(SLOTS // BLOCK,),
        in_specs=[pl.BlockSpec(x.shape, whole) for x in (arrived, bias, valid)],
        out_specs=pl.BlockSpec((BLOCK, GROUP * HD), lambda s: (s, 0)),
        scratch_shapes=[
            pltpu.VMEM((TILES, SLOTS, LANES), jnp.bfloat16),
            pltpu.VMEM((BLOCK, BLOCK), jnp.float32),
        ],
        compiler_params=pltpu.CompilerParams(vmem_limit_bytes=VMEM),
        name="prefill",
    )(arrived, bias, valid)


def exchanged(array, distance):
    found = jnp.zeros_like(array)
    for bit in range(N_INST.bit_length() - 1):
        pairs = [(i, i ^ 1 << bit) for i in range(N_INST)]
        found = jnp.where(distance == 1 << bit, lax.ppermute(array, "inst", pairs), found)
    return found


def local(
    step_queries,
    step_keyvals,
    cache_pages,
    block_table,
    context_len,
    partner,
    moved_slot,
    prompt_queries,
    prompt_keyvals,
    prompt_target,
):
    inst = lax.axis_index("inst")
    device = inst * N_TP + lax.axis_index("tp")
    targets = prompt_target.reshape(-1, LANES)
    sent = dispatch(
        device[None], targets, prompt_queries, prompt_keyvals.reshape(ROWS_DEV * KVH, 2 * HD)
    )
    arrived = lax.all_to_all(
        sent.reshape(N_INST * N_TP, MESSAGE // 4, 4, LANES), ("inst", "tp"), 0, 0, tiled=True
    ).reshape(sent.shape)

    moved = moved_slot[inst]
    distance = inst ^ partner[inst]
    queries = step_queries.reshape(STEPS * REQ, GROUP * HD)
    fresh = step_keyvals.reshape(STEPS * REQ, 2 * HD)
    traded = jnp.concatenate(
        [
            lax.dynamic_index_in_dim(step_queries, moved, 1, keepdims=False),
            lax.dynamic_index_in_dim(step_keyvals[:, :, 0], moved, 1, keepdims=False),
        ],
        axis=1,
    )
    came = exchanged(traded, distance)
    info = jnp.stack([inst, moved])
    decoded, bias, valid = decode(
        info, context_len, block_table, queries, fresh, came,
        cache_pages.reshape(POOL * PAGE, 2 * HD), targets,
    )
    decoded = decoded.reshape(STEPS, REQ, GROUP * HD)
    back = exchanged(lax.dynamic_index_in_dim(decoded, moved, 1, keepdims=False), distance)
    here = (jnp.arange(REQ, dtype=jnp.int32) == moved)[None, :, None]
    decode_output = jnp.where(here, back[:, None, :], decoded)
    return decode_output, prefill(arrived, bias, valid)


def solution(mesh):
    placed = (
        P(None, "inst", "tp"),
        P(None, "inst", "tp", None),
        P("inst", None, "tp", None),
        P("inst", None),
        P(),
        P(),
        P(),
        P(("inst", "tp"), None),
        P(("inst", "tp"), None, None),
        P(),
    )
    return jax.shard_map(
        local,
        mesh=mesh,
        in_specs=placed,
        out_specs=(P(None, "inst", "tp"), P("inst", "tp")),
        check_vma=False,
    )
```

```python
import functools
import math

import jax
import jax.numpy as jnp
from jax import lax
from jax.experimental import pallas as pl
from jax.experimental.pallas import tpu as pltpu
from jax.sharding import PartitionSpec as P

H, KVH, HD = 64, 8, 128
REQ, PAGE, MAXP, STEPS = 8, 16, 16, 4
ROWS_DEV, CTX, POOL, CAP, SLOTS = 64, 256, 128, 2, 1024
N_INST, N_TP = 64, 8
GROUP = H // KVH
TILES = GROUP + 2
MESSAGE = TILES * CAP
LANES = 128
LOG2_SCALE = HD**-0.5 * math.log2(math.e)
MASKED = -1e30
VMEM = 48 * 1024 * 1024


def iota(shape, dim):
    return lax.broadcasted_iota(jnp.int32, shape, dim)


def dot(a, b, contract=((1,), (0,))):
    return lax.dot_general(a, b, (contract, ((), ())), preferred_element_type=jnp.float32)


NT = ((1,), (1,))


INSTS = 8


def dispatch_kernel(me_ref, target_ref, queries_ref, keyvals_ref, out_ref, place_ref, rows_ref):
    step = pl.program_id(0)

    @pl.when(step == 0)
    def _():
        me = me_ref[0]
        line = lax.rem(lax.div(me, 2), 8)
        both = jnp.sum(
            jnp.where(iota((8, LANES), 0) == line, target_ref[...], 0), axis=0, keepdims=True
        )
        both = jnp.broadcast_to(both, (8, LANES))
        other = pltpu.roll(both, ROWS_DEV, 1)
        first = iota((8, LANES), 1) < ROWS_DEV
        odd = lax.rem(me, 2) == 1
        mine = jnp.where(first != odd, both, other)[0:1]
        down, along = iota((ROWS_DEV, LANES), 0), iota((ROWS_DEV, LANES), 1)
        wide = jnp.broadcast_to(mine, (ROWS_DEV, LANES))
        column = jnp.sum(jnp.where(down == along, wide, 0), axis=1, keepdims=True)
        earlier = (column == wide) & (down < along % ROWS_DEV)
        rank = jnp.sum(earlier.astype(jnp.int32), axis=0, keepdims=True)
        place = jnp.broadcast_to(mine * CAP + rank, (8, LANES))
        for i in range(4):
            place_ref[:, i * LANES : (i + 1) * LANES] = place
        down, along = iota((512, 512), 0), iota((512, 512), 1)
        order = (down % ROWS_DEV == along // KVH) & (down // ROWS_DEV == along % KVH)
        keyvals = dot(order.astype(jnp.float32).astype(jnp.bfloat16), keyvals_ref[...])
        keyvals = keyvals.astype(jnp.bfloat16)
        for c in range(N_TP * TILES):
            tp, tile = divmod(c, TILES)
            if tile < GROUP:
                piece = queries_ref[:, (tp * GROUP + tile) * HD : (tp * GROUP + tile + 1) * HD]
            else:
                lane = (tile - GROUP) * HD
                piece = keyvals[tp * ROWS_DEV : (tp + 1) * ROWS_DEV, lane : lane + HD]
            to, col = c % 8, c // 8
            rows_ref[to * ROWS_DEV : (to + 1) * ROWS_DEV, col * LANES : (col + 1) * LANES] = piece

    down, along = iota((LANES, 512), 0), iota((LANES, 512), 1)
    wanted = (step * INSTS + down // 16) * CAP + down % 2
    place = jnp.broadcast_to(place_ref[0:1, :], (LANES, 512))
    chosen = (place == wanted) & (along // ROWS_DEV == down // 2 % 8)
    out = dot(chosen.astype(jnp.float32).astype(jnp.bfloat16), rows_ref[...])
    out = out.astype(jnp.bfloat16)
    for i in range(INSTS):
        for col in range(TILES):
            out_ref[i * 160 + col * 16 : i * 160 + (col + 1) * 16, :] = out[
                i * 16 : (i + 1) * 16, col * LANES : (col + 1) * LANES
            ]


def dispatch(me, targets, queries, keyvals):
    rows = N_INST * N_TP * MESSAGE
    return pl.pallas_call(
        dispatch_kernel,
        out_shape=pltpu.HBM((rows, LANES), jnp.bfloat16),
        grid_spec=pltpu.PrefetchScalarGridSpec(
            num_scalar_prefetch=1,
            grid=(N_INST // INSTS,),
            in_specs=[
                pl.BlockSpec((8, LANES), lambda s, me: (me[0] // 16, 0)),
                pl.BlockSpec((ROWS_DEV, H * HD), lambda s, me: (0, 0)),
                pl.BlockSpec((ROWS_DEV * KVH, 2 * HD), lambda s, me: (0, 0)),
            ],
            out_specs=pl.BlockSpec((rows * INSTS // N_INST, LANES), lambda s, me: (s, 0)),
            scratch_shapes=[
                pltpu.VMEM((8, 512), jnp.int32),
                pltpu.VMEM((512, TILES * LANES), jnp.bfloat16),
            ],
        ),
        compiler_params=pltpu.CompilerParams(vmem_limit_bytes=VMEM),
        name="dispatch",
    )(me, *(pltpu.with_memory_space_constraint(x, pltpu.HBM) for x in (targets, queries, keyvals)))


def prepare_kernel(
    inst_ref, slot_ref, table_ref, cache_ref, target_ref, leaving_ref, context_ref, mask_ref
):
    inst = inst_ref[0]
    moved = slot_ref[inst]
    for r in range(REQ):
        for j in range(MAXP):
            page = pl.multiple_of(table_ref[r, j] * PAGE, PAGE)
            row = r * CTX + j * PAGE
            context_ref[row : row + PAGE, :] = cache_ref[pl.ds(page, PAGE), :]
    leaving_ref[...] = context_ref[pl.ds(pl.multiple_of(moved * CTX, CTX), CTX), :]
    lines = target_ref.shape[0]
    hits = (target_ref[...] == inst).astype(jnp.float32).astype(jnp.bfloat16)
    slot, along = iota((SLOTS, lines), 0), iota((SLOTS, lines), 1)
    spread = dot((slot // 4 == along).astype(jnp.float32).astype(jnp.bfloat16), hits)
    slot, along = iota((SLOTS, LANES), 0), iota((SLOTS, LANES), 1)
    spread = jnp.where(along // ROWS_DEV == slot // 2 % 2, spread, 0.0).astype(jnp.bfloat16)
    count = dot(spread, jnp.ones((LANES, LANES), jnp.bfloat16))
    mask = jnp.where(count > (slot % 2).astype(jnp.float32), 0.0, MASKED)
    mask_ref[...] = mask.astype(jnp.bfloat16)


def specs(*spaces):
    return [pl.BlockSpec(memory_space=s) for s in spaces]


def prepare(inst, slots, table, cache, targets):
    smem, vmem = pltpu.SMEM, pltpu.VMEM
    return pl.pallas_call(
        prepare_kernel,
        out_shape=(
            jax.ShapeDtypeStruct((CTX, 2 * HD), jnp.bfloat16),
            jax.ShapeDtypeStruct((REQ * CTX, 2 * HD), jnp.bfloat16),
            jax.ShapeDtypeStruct((SLOTS, LANES), jnp.bfloat16),
        ),
        in_specs=specs(smem, smem, smem, vmem, vmem),
        out_specs=specs(vmem, vmem, vmem),
        compiler_params=pltpu.CompilerParams(vmem_limit_bytes=VMEM),
        name="prepare",
    )(inst, slots, table, cache, targets)


BITS = N_INST.bit_length() - 1


def decode_kernel(
    inst_ref, partner_ref, slot_ref, lens_ref, queries_ref, fresh_ref, context_ref, *refs
):
    *came_refs, out_ref, came_ref = refs
    inst = inst_ref[0]
    other = partner_ref[inst]
    moved = slot_ref[inst]
    for bit in range(BITS):

        @pl.when(jnp.bitwise_xor(inst, other) == 1 << bit)
        def _(bit=bit):
            came_ref[...] = came_refs[bit][...]

    rows = STEPS * REQ
    queries, fresh, came = queries_ref[...], fresh_ref[...], came_ref[...]
    query = jnp.concatenate([queries[:, g * HD : (g + 1) * HD] for g in range(GROUP)], axis=0)
    n = GROUP * rows
    row = iota((n, 1), 0)
    request, moment = row % REQ, row // REQ % STEPS
    newer = dot(query, fresh[:, :HD], NT)
    along = iota((n, rows), 1)
    newer = jnp.where((along % REQ == request) & (along // REQ <= moment), newer, MASKED)
    past = jnp.zeros((n, CTX), jnp.float32)
    length = jnp.zeros((n, 1), jnp.int32)
    values = []
    for r in range(REQ):
        context = jnp.where(moved == r, came, context_ref[r * CTX : (r + 1) * CTX, :])
        values.append(context[:, HD:])
        past = jnp.where(request == r, dot(query, context[:, :HD], NT), past)
        source = jnp.where(moved == r, other * REQ + slot_ref[other], inst * REQ + r)
        length = jnp.where(request == r, lens_ref[source], length)
    past = jnp.where(iota((n, CTX), 1) < length, past, MASKED)
    top = jnp.maximum(
        jnp.max(past, axis=1, keepdims=True), jnp.max(newer, axis=1, keepdims=True)
    )
    past = jnp.exp2((past - top) * LOG2_SCALE)
    newer = jnp.exp2((newer - top) * LOG2_SCALE)
    total = jnp.sum(past, axis=1, keepdims=True) + jnp.sum(newer, axis=1, keepdims=True)
    past, newer = past / total, newer / total
    out = dot(newer.astype(jnp.bfloat16), fresh[:, HD:])
    for r in range(REQ):
        weights = jnp.where(request == r, past, 0.0).astype(jnp.bfloat16)
        out = out + dot(weights, values[r])
    for g in range(GROUP):
        out_ref[:, g * HD : (g + 1) * HD] = out[g * rows : (g + 1) * rows].astype(jnp.bfloat16)


def decode(inst, partner, slots, lens, queries, fresh, context, came):
    smem, vmem = pltpu.SMEM, pltpu.VMEM
    return pl.pallas_call(
        decode_kernel,
        out_shape=jax.ShapeDtypeStruct(queries.shape, jnp.bfloat16),
        in_specs=specs(*[smem] * 4, *[vmem] * (3 + BITS)),
        out_specs=specs(vmem)[0],
        scratch_shapes=[pltpu.VMEM((CTX, 2 * HD), jnp.bfloat16)],
        compiler_params=pltpu.CompilerParams(vmem_limit_bytes=VMEM),
        name="decode",
    )(inst, partner, slots, lens, queries, fresh, context, *came)


BLOCK = 128


def prefill_kernel(arrived_ref, mask_ref, out_ref, packed_ref, keys_ref, last_ref):
    size = N_TP * MESSAGE
    to, src = iota((size, size), 0), iota((size, size), 1)
    order = (
        (to // 16 == src // 2 % TILES) & (to // 2 % 8 == src // MESSAGE) & (to % 2 == src % 2)
    )
    order = order.astype(jnp.float32).astype(jnp.bfloat16)
    for i in range(0, N_INST, 8):
        rows = jnp.concatenate(
            [arrived_ref[(i + j) * size : (i + j + 1) * size, :] for j in range(8)], axis=1
        )
        rows = dot(order, rows).astype(jnp.bfloat16)
        for tile in range(TILES):
            for j in range(8):
                packed_ref[tile, (i + j) * 16 : (i + j + 1) * 16, :] = rows[
                    tile * 16 : (tile + 1) * 16, j * LANES : (j + 1) * LANES
                ]
    mask = mask_ref[...].astype(jnp.float32)
    late = iota((SLOTS, BLOCK), 0) % BLOCK > iota((SLOTS, BLOCK), 1)
    keys_ref[:, :HD] = packed_ref[GROUP]
    keys_ref[:, HD:] = mask_ref[...]
    last_ref[:, :HD] = packed_ref[GROUP]
    last_ref[:, HD:] = jnp.where(late, MASKED, mask).astype(jnp.bfloat16)
    position = iota((BLOCK, BLOCK), 0) == iota((BLOCK, BLOCK), 1)
    position = position.astype(jnp.float32).astype(jnp.bfloat16)
    positions = jnp.concatenate([position] * GROUP, axis=0)
    for start in range(0, SLOTS, BLOCK):
        end = start + BLOCK
        filled = (mask_ref[start:end, 0:1].astype(jnp.float32) == 0).astype(jnp.float32)
        filled = jnp.concatenate([filled] * GROUP, axis=0)
        query = jnp.concatenate([packed_ref[h, start:end, :] for h in range(GROUP)], axis=0)
        query = jnp.concatenate([query, positions], axis=1)
        scores = dot(query, last_ref[start:end, :], NT)
        if start:
            scores = jnp.concatenate([dot(query, keys_ref[:start, :], NT), scores], axis=1)
        top = jnp.max(scores, axis=1, keepdims=True)
        expo = jnp.exp2((scores - top) * LOG2_SCALE).astype(jnp.bfloat16)
        ones = jnp.ones((end, LANES), jnp.bfloat16)
        out = dot(expo, jnp.concatenate([packed_ref[GROUP + 1, :end, :], ones], axis=1))
        out = (out[:, :HD] * (filled / out[:, HD:])).astype(jnp.bfloat16)
        for h in range(GROUP):
            out_ref[start:end, h * HD : (h + 1) * HD] = out[h * BLOCK : (h + 1) * BLOCK]


def prefill(arrived, mask):
    vmem = pltpu.VMEM
    return pl.pallas_call(
        prefill_kernel,
        out_shape=jax.ShapeDtypeStruct((SLOTS, GROUP * HD), jnp.bfloat16),
        in_specs=specs(vmem, vmem),
        out_specs=specs(vmem)[0],
        scratch_shapes=[
            pltpu.VMEM((TILES, SLOTS, LANES), jnp.bfloat16),
            pltpu.VMEM((SLOTS, 2 * HD), jnp.bfloat16),
            pltpu.VMEM((SLOTS, 2 * HD), jnp.bfloat16),
        ],
        compiler_params=pltpu.CompilerParams(vmem_limit_bytes=VMEM),
        name="prefill",
    )(arrived, mask)


def local(
    step_queries,
    step_keyvals,
    cache_pages,
    block_table,
    context_len,
    partner,
    moved_slot,
    prompt_queries,
    prompt_keyvals,
    prompt_target,
):
    inst = lax.axis_index("inst")
    device = inst * N_TP + lax.axis_index("tp")
    targets = prompt_target.reshape(-1, LANES)
    sent = dispatch(
        device[None], targets, prompt_queries, prompt_keyvals.reshape(ROWS_DEV * KVH, 2 * HD)
    )
    arrived = lax.all_to_all(
        sent.reshape(N_INST * N_TP, MESSAGE // 4, 4, LANES), ("inst", "tp"), 0, 0, tiled=True
    ).reshape(sent.shape)

    cache = cache_pages.reshape(POOL * PAGE, 2 * HD)
    leaving, context, mask = prepare(inst[None], moved_slot, block_table, cache, targets)
    came = [
        lax.ppermute(leaving, "inst", [(i, i ^ 1 << bit) for i in range(N_INST)])
        for bit in range(BITS)
    ]
    prefill_output = prefill(arrived, mask)
    step_queries, prefill_output = lax.optimization_barrier((step_queries, prefill_output))
    decode_output = decode(
        inst[None], partner, moved_slot, context_len,
        step_queries.reshape(STEPS * REQ, GROUP * HD),
        step_keyvals.reshape(STEPS * REQ, 2 * HD), context, came,
    )
    return decode_output.reshape(step_queries.shape), prefill_output


def solution(mesh):
    placed = (
        P(None, "inst", "tp"),
        P(None, "inst", "tp", None),
        P("inst", None, "tp", None),
        P("inst", None),
        P(),
        P(),
        P(),
        P(("inst", "tp"), None),
        P(("inst", "tp"), None, None),
        P(),
    )
    return jax.shard_map(
        local,
        mesh=mesh,
        in_specs=placed,
        out_specs=(P(None, "inst", "tp"), P("inst", "tp")),
        check_vma=False,
    )
```

```python
import functools
import math

import jax
import jax.numpy as jnp
from jax import lax
from jax.experimental import pallas as pl
from jax.experimental.pallas import tpu as pltpu
from jax.sharding import PartitionSpec as P

H, KVH, HD = 64, 8, 128
REQ, PAGE, MAXP, STEPS = 8, 16, 16, 4
ROWS_DEV, CTX, POOL, CAP, SLOTS = 64, 256, 128, 2, 1024
N_INST, N_TP = 64, 8
GROUP = H // KVH
TILES = GROUP + 2
MESSAGE = TILES * CAP
LANES = 128
LOG2_SCALE = HD**-0.5 * math.log2(math.e)
MASKED = -1e30
VMEM = 48 * 1024 * 1024


def iota(shape, dim):
    return lax.broadcasted_iota(jnp.int32, shape, dim)


def dot(a, b, contract=((1,), (0,))):
    return lax.dot_general(a, b, (contract, ((), ())), preferred_element_type=jnp.float32)


NT = ((1,), (1,))


INSTS = 32


def dispatch_kernel(me_ref, target_ref, queries_ref, keyvals_ref, out_ref, place_ref, rows_ref):
    step = pl.program_id(0)

    @pl.when(step == 0)
    def _():
        me = me_ref[0]
        line = lax.rem(lax.div(me, 2), 8)
        both = jnp.sum(
            jnp.where(iota((8, LANES), 0) == line, target_ref[...], 0), axis=0, keepdims=True
        )
        both = jnp.broadcast_to(both, (8, LANES))
        other = pltpu.roll(both, ROWS_DEV, 1)
        first = iota((8, LANES), 1) < ROWS_DEV
        odd = lax.rem(me, 2) == 1
        mine = jnp.where(first != odd, both, other)[0:1]
        down, along = iota((ROWS_DEV, LANES), 0), iota((ROWS_DEV, LANES), 1)
        wide = jnp.broadcast_to(mine, (ROWS_DEV, LANES))
        column = jnp.sum(jnp.where(down == along, wide, 0), axis=1, keepdims=True)
        earlier = (column == wide) & (down < along % ROWS_DEV)
        rank = jnp.sum(earlier.astype(jnp.int32), axis=0, keepdims=True)
        place = jnp.broadcast_to(mine * CAP + rank, (8, LANES))
        for i in range(4):
            place_ref[:, i * LANES : (i + 1) * LANES] = place
        down, along = iota((512, 512), 0), iota((512, 512), 1)
        order = (down % ROWS_DEV == along // KVH) & (down // ROWS_DEV == along % KVH)
        keyvals = dot(order.astype(jnp.float32).astype(jnp.bfloat16), keyvals_ref[...])
        keyvals = keyvals.astype(jnp.bfloat16)
        for c in range(N_TP * TILES):
            tp, tile = divmod(c, TILES)
            if tile < GROUP:
                piece = queries_ref[:, (tp * GROUP + tile) * HD : (tp * GROUP + tile + 1) * HD]
            else:
                lane = (tile - GROUP) * HD
                piece = keyvals[tp * ROWS_DEV : (tp + 1) * ROWS_DEV, lane : lane + HD]
            to, col = c % 8, c // 8
            rows_ref[to * ROWS_DEV : (to + 1) * ROWS_DEV, col * LANES : (col + 1) * LANES] = piece

    down, along = iota((INSTS * 16, 512), 0), iota((INSTS * 16, 512), 1)
    wanted = (step * INSTS + down // 16) * CAP + down % 2
    place = jnp.broadcast_to(place_ref[0:1, :], (INSTS * 16, 512))
    chosen = (place == wanted) & (along // ROWS_DEV == down // 2 % 8)
    out = dot(chosen.astype(jnp.float32).astype(jnp.bfloat16), rows_ref[...])
    out = out.astype(jnp.bfloat16)
    for i in range(INSTS):
        for col in range(TILES):
            out_ref[i * 160 + col * 16 : i * 160 + (col + 1) * 16, :] = out[
                i * 16 : (i + 1) * 16, col * LANES : (col + 1) * LANES
            ]


def dispatch(me, targets, queries, keyvals):
    rows = N_INST * N_TP * MESSAGE
    return pl.pallas_call(
        dispatch_kernel,
        out_shape=pltpu.HBM((rows, LANES), jnp.bfloat16),
        grid_spec=pltpu.PrefetchScalarGridSpec(
            num_scalar_prefetch=1,
            grid=(N_INST // INSTS,),
            in_specs=[
                pl.BlockSpec((8, LANES), lambda s, me: (me[0] // 16, 0)),
                pl.BlockSpec((ROWS_DEV, H * HD), lambda s, me: (0, 0)),
                pl.BlockSpec((ROWS_DEV * KVH, 2 * HD), lambda s, me: (0, 0)),
            ],
            out_specs=pl.BlockSpec((rows * INSTS // N_INST, LANES), lambda s, me: (s, 0)),
            scratch_shapes=[
                pltpu.VMEM((8, 512), jnp.int32),
                pltpu.VMEM((512, TILES * LANES), jnp.bfloat16),
            ],
        ),
        compiler_params=pltpu.CompilerParams(vmem_limit_bytes=VMEM),
        name="dispatch",
    )(me, *(pltpu.with_memory_space_constraint(x, pltpu.HBM) for x in (targets, queries, keyvals)))


def prepare_kernel(
    inst_ref, slot_ref, table_ref, cache_ref, target_ref, leaving_ref, context_ref, mask_ref
):
    inst = inst_ref[0]
    moved = slot_ref[inst]
    for r in range(REQ):
        for j in range(MAXP):
            page = pl.multiple_of(table_ref[r, j] * PAGE, PAGE)
            row = r * CTX + j * PAGE
            context_ref[row : row + PAGE, :] = cache_ref[pl.ds(page, PAGE), :]
    leaving_ref[...] = context_ref[pl.ds(pl.multiple_of(moved * CTX, CTX), CTX), :]
    lines = target_ref.shape[0]
    hits = (target_ref[...] == inst).astype(jnp.float32).astype(jnp.bfloat16)
    slot, along = iota((SLOTS, lines), 0), iota((SLOTS, lines), 1)
    spread = dot((slot // 4 == along).astype(jnp.float32).astype(jnp.bfloat16), hits)
    slot, along = iota((SLOTS, LANES), 0), iota((SLOTS, LANES), 1)
    spread = jnp.where(along // ROWS_DEV == slot // 2 % 2, spread, 0.0).astype(jnp.bfloat16)
    count = dot(spread, jnp.ones((LANES, LANES), jnp.bfloat16))
    mask = jnp.where(count > (slot % 2).astype(jnp.float32), 0.0, MASKED)
    mask_ref[...] = mask.astype(jnp.bfloat16)


def specs(*spaces):
    return [pl.BlockSpec(memory_space=s) for s in spaces]


def prepare(inst, slots, table, cache, targets):
    smem, vmem = pltpu.SMEM, pltpu.VMEM
    return pl.pallas_call(
        prepare_kernel,
        out_shape=(
            jax.ShapeDtypeStruct((CTX, 2 * HD), jnp.bfloat16),
            jax.ShapeDtypeStruct((REQ * CTX, 2 * HD), jnp.bfloat16),
            jax.ShapeDtypeStruct((SLOTS, LANES), jnp.bfloat16),
        ),
        in_specs=specs(smem, smem, smem, vmem, vmem),
        out_specs=specs(vmem, vmem, vmem),
        compiler_params=pltpu.CompilerParams(vmem_limit_bytes=VMEM),
        name="prepare",
    )(inst, slots, table, cache, targets)


def decode_kernel(inst_ref, lens_ref, queries_ref, fresh_ref, context_ref, out_ref):
    inst = inst_ref[0]
    rows = STEPS * REQ
    queries, fresh = queries_ref[...], fresh_ref[...]
    query = jnp.concatenate([queries[:, g * HD : (g + 1) * HD] for g in range(GROUP)], axis=0)
    n = GROUP * rows
    row = iota((n, 1), 0)
    request, moment = row % REQ, row // REQ % STEPS
    newer = dot(query, fresh[:, :HD], NT)
    along = iota((n, rows), 1)
    newer = jnp.where((along % REQ == request) & (along // REQ <= moment), newer, MASKED)
    past = jnp.zeros((n, CTX), jnp.float32)
    length = jnp.zeros((n, 1), jnp.int32)
    for r in range(REQ):
        keys = context_ref[r * CTX : (r + 1) * CTX, :HD]
        past = jnp.where(request == r, dot(query, keys, NT), past)
        length = jnp.where(request == r, lens_ref[inst * REQ + r], length)
    past = jnp.where(iota((n, CTX), 1) < length, past, MASKED)
    past, newer = shares(past, newer)
    out = dot(newer.astype(jnp.bfloat16), fresh[:, HD:])
    for r in range(REQ):
        weights = jnp.where(request == r, past, 0.0).astype(jnp.bfloat16)
        out = out + dot(weights, context_ref[r * CTX : (r + 1) * CTX, HD:])
    for g in range(GROUP):
        out_ref[:, g * HD : (g + 1) * HD] = out[g * rows : (g + 1) * rows].astype(jnp.bfloat16)


def shares(past, newer):
    top = jnp.maximum(
        jnp.max(past, axis=1, keepdims=True), jnp.max(newer, axis=1, keepdims=True)
    )
    past = jnp.exp2((past - top) * LOG2_SCALE)
    newer = jnp.exp2((newer - top) * LOG2_SCALE)
    total = jnp.sum(past, axis=1, keepdims=True) + jnp.sum(newer, axis=1, keepdims=True)
    return past / total, newer / total


def decode(inst, lens, queries, fresh, context):
    smem, vmem = pltpu.SMEM, pltpu.VMEM
    return pl.pallas_call(
        decode_kernel,
        out_shape=jax.ShapeDtypeStruct(queries.shape, jnp.bfloat16),
        in_specs=specs(smem, smem, vmem, vmem, vmem),
        out_specs=specs(vmem)[0],
        compiler_params=pltpu.CompilerParams(vmem_limit_bytes=VMEM),
        name="decode",
    )(inst, lens, queries, fresh, context)


BITS = N_INST.bit_length() - 1


def traded_kernel(
    inst_ref, partner_ref, slot_ref, lens_ref, queries_ref, fresh_ref, decoded_ref, *refs
):
    *came_refs, out_ref = refs
    inst = inst_ref[0]
    other = partner_ref[inst]
    moved = slot_ref[inst]
    distance = jnp.bitwise_xor(inst, other)
    came = came_refs[0][...]
    for bit in range(1, BITS):
        came = jnp.where(distance == 1 << bit, came_refs[bit][...], came)
    rows = STEPS * REQ
    chosen = iota((8, rows), 1) == iota((8, rows), 0) * REQ + moved
    chosen = chosen.astype(jnp.float32).astype(jnp.bfloat16)
    queries = dot(chosen, queries_ref[...])
    fresh = dot(chosen, fresh_ref[...]).astype(jnp.bfloat16)
    query = jnp.concatenate([queries[:, g * HD : (g + 1) * HD] for g in range(GROUP)], axis=0)
    query = query.astype(jnp.bfloat16)
    n = GROUP * 8
    newer = dot(query, fresh[:, :HD], NT)
    moment, along = iota((n, 8), 0) % 8, iota((n, 8), 1)
    newer = jnp.where((along <= moment) & (along < STEPS), newer, MASKED)
    length = lens_ref[other * REQ + slot_ref[other]]
    past = jnp.where(iota((n, CTX), 1) < length, dot(query, came[:, :HD], NT), MASKED)
    past, newer = shares(past, newer)
    out = dot(past.astype(jnp.bfloat16), came[:, HD:])
    out = out + dot(newer.astype(jnp.bfloat16), fresh[:, HD:])
    out = jnp.concatenate([out[g * 8 : (g + 1) * 8] for g in range(GROUP)], axis=1)
    out = dot(chosen, out.astype(jnp.bfloat16), ((0,), (0,)))
    here = iota((rows, 1), 0) % REQ == moved
    out_ref[...] = jnp.where(here, out, decoded_ref[...].astype(jnp.float32)).astype(jnp.bfloat16)


def traded(inst, partner, slots, lens, queries, fresh, decoded, came):
    smem, vmem = pltpu.SMEM, pltpu.VMEM
    return pl.pallas_call(
        traded_kernel,
        out_shape=jax.ShapeDtypeStruct(queries.shape, jnp.bfloat16),
        in_specs=specs(*[smem] * 4, *[vmem] * (3 + BITS)),
        out_specs=specs(vmem)[0],
        compiler_params=pltpu.CompilerParams(vmem_limit_bytes=VMEM),
        name="traded",
    )(inst, partner, slots, lens, queries, fresh, decoded, *came)


BLOCK = 128
HEADS = 4


def prefill_kernel(arrived_ref, mask_ref, out_ref, packed_ref, keys_ref, last_ref, values_ref):
    size = N_TP * MESSAGE
    to, src = iota((size, size), 0), iota((size, size), 1)
    order = (
        (to // 16 == src // 2 % TILES) & (to // 2 % 8 == src // MESSAGE) & (to % 2 == src % 2)
    )
    order = order.astype(jnp.float32).astype(jnp.bfloat16)
    late = iota((BLOCK, BLOCK), 0) > iota((BLOCK, BLOCK), 1)
    position = iota((BLOCK, BLOCK), 0) == iota((BLOCK, BLOCK), 1)
    position = position.astype(jnp.float32).astype(jnp.bfloat16)
    positions = jnp.concatenate([position] * HEADS, axis=0)

    def bring(start, end):
        first = start // 16
        rows = jnp.concatenate(
            [arrived_ref[(first + j) * size : (first + j + 1) * size, :] for j in range(8)], axis=1
        )
        rows = dot(order, rows).astype(jnp.bfloat16)
        for tile in range(TILES):
            for j in range(8):
                packed_ref[tile, start + j * 16 : start + (j + 1) * 16, :] = rows[
                    tile * 16 : (tile + 1) * 16, j * LANES : (j + 1) * LANES
                ]
        mask = mask_ref[start:end, :]
        keys_ref[start:end, :HD] = packed_ref[GROUP, start:end, :]
        keys_ref[start:end, HD:] = mask
        last_ref[start:end, :HD] = packed_ref[GROUP, start:end, :]
        mask = jnp.where(late, MASKED, mask.astype(jnp.float32))
        last_ref[start:end, HD:] = mask.astype(jnp.bfloat16)
        values_ref[start:end, :HD] = packed_ref[GROUP + 1, start:end, :]
        values_ref[start:end, HD:] = jnp.ones((BLOCK, LANES), jnp.bfloat16)

    def scored(start, end, heads):
        if heads[0] == 0:
            bring(start, end)
        query = jnp.concatenate([packed_ref[h, start:end, :] for h in heads], axis=0)
        query = jnp.concatenate([query, positions], axis=1)
        scores = dot(query, last_ref[start:end, :], NT)
        if start:
            scores = jnp.concatenate([dot(query, keys_ref[:start, :], NT), scores], axis=1)
        return scores

    work = [
        (start, start + BLOCK, range(h, h + HEADS))
        for start in range(0, SLOTS, BLOCK)
        for h in range(0, GROUP, HEADS)
    ]
    scores = scored(*work[0])
    for i, (start, end, heads) in enumerate(work):
        ahead = scored(*work[i + 1]) if i + 1 < len(work) else None
        filled = (mask_ref[start:end, 0:1].astype(jnp.float32) == 0).astype(jnp.float32)
        filled = jnp.concatenate([filled] * HEADS, axis=0)
        top = jnp.max(scores, axis=1, keepdims=True)
        expo = jnp.exp2((scores - top) * LOG2_SCALE).astype(jnp.bfloat16)
        out = dot(expo, values_ref[:end, :])
        out = (out[:, :HD] * (filled / out[:, HD:])).astype(jnp.bfloat16)
        for j, h in enumerate(heads):
            out_ref[start:end, h * HD : (h + 1) * HD] = out[j * BLOCK : (j + 1) * BLOCK]
        scores = ahead


def prefill(arrived, mask):
    vmem = pltpu.VMEM
    return pl.pallas_call(
        prefill_kernel,
        out_shape=jax.ShapeDtypeStruct((SLOTS, GROUP * HD), jnp.bfloat16),
        in_specs=specs(vmem, vmem),
        out_specs=specs(vmem)[0],
        scratch_shapes=[
            pltpu.VMEM((TILES, SLOTS, LANES), jnp.bfloat16),
            pltpu.VMEM((SLOTS, 2 * HD), jnp.bfloat16),
            pltpu.VMEM((SLOTS, 2 * HD), jnp.bfloat16),
            pltpu.VMEM((SLOTS, 2 * HD), jnp.bfloat16),
        ],
        compiler_params=pltpu.CompilerParams(vmem_limit_bytes=VMEM),
        name="prefill",
    )(arrived, mask)


def local(
    step_queries,
    step_keyvals,
    cache_pages,
    block_table,
    context_len,
    partner,
    moved_slot,
    prompt_queries,
    prompt_keyvals,
    prompt_target,
):
    inst = lax.axis_index("inst")
    device = inst * N_TP + lax.axis_index("tp")
    targets = prompt_target.reshape(-1, LANES)
    sent = dispatch(
        device[None], targets, prompt_queries, prompt_keyvals.reshape(ROWS_DEV * KVH, 2 * HD)
    )
    arrived = lax.all_to_all(
        sent.reshape(N_INST * N_TP, MESSAGE // 4, 4, LANES), ("inst", "tp"), 0, 0, tiled=True
    ).reshape(sent.shape)

    cache = cache_pages.reshape(POOL * PAGE, 2 * HD)
    leaving, context, mask = prepare(inst[None], moved_slot, block_table, cache, targets)
    queries = step_queries.reshape(STEPS * REQ, GROUP * HD)
    fresh = step_keyvals.reshape(STEPS * REQ, 2 * HD)
    decoded = decode(inst[None], context_len, queries, fresh, context)
    leaving, decoded = lax.optimization_barrier((leaving, decoded))
    came = [
        lax.ppermute(leaving, "inst", [(i, i ^ 1 << bit) for i in range(N_INST)])
        for bit in range(BITS)
    ]
    prefill_output = prefill(arrived, mask)
    queries, prefill_output = lax.optimization_barrier((queries, prefill_output))
    decoded = traded(inst[None], partner, moved_slot, context_len, queries, fresh, decoded, came)
    return decoded.reshape(step_queries.shape), prefill_output


def solution(mesh):
    placed = (
        P(None, "inst", "tp"),
        P(None, "inst", "tp", None),
        P("inst", None, "tp", None),
        P("inst", None),
        P(),
        P(),
        P(),
        P(("inst", "tp"), None),
        P(("inst", "tp"), None, None),
        P(),
    )
    return jax.shard_map(
        local,
        mesh=mesh,
        in_specs=placed,
        out_specs=(P(None, "inst", "tp"), P("inst", "tp")),
        check_vma=False,
    )
```

```python
import functools
import math

import jax
import jax.numpy as jnp
from jax import lax
from jax.experimental import pallas as pl
from jax.experimental.pallas import tpu as pltpu
from jax.sharding import PartitionSpec as P

H, KVH, HD = 64, 8, 128
REQ, PAGE, MAXP, STEPS = 8, 16, 16, 4
ROWS_DEV, CTX, POOL, CAP, SLOTS = 64, 256, 128, 2, 1024
N_INST, N_TP = 64, 8
GROUP = H // KVH
TILES = GROUP + 2
MESSAGE = TILES * CAP
LANES = 128
LOG2_SCALE = HD**-0.5 * math.log2(math.e)
MASKED = -1e30
VMEM = 48 * 1024 * 1024


def iota(shape, dim):
    return lax.broadcasted_iota(jnp.int32, shape, dim)


def dot(a, b, contract=((1,), (0,))):
    return lax.dot_general(a, b, (contract, ((), ())), preferred_element_type=jnp.float32)


NT = ((1,), (1,))


INSTS = 16


def dispatch_kernel(
    me_ref, target_ref, queries_ref, keyvals_ref, out_hbm, rows_ref, out_ref, sems
):
    me = me_ref[0]
    line = lax.rem(lax.div(me, 2), 8)
    both = jnp.sum(
        jnp.where(iota((8, LANES), 0) == line, target_ref[...], 0), axis=0, keepdims=True
    )
    both = jnp.broadcast_to(both, (8, LANES))
    other = pltpu.roll(both, ROWS_DEV, 1)
    first = iota((8, LANES), 1) < ROWS_DEV
    odd = lax.rem(me, 2) == 1
    mine = jnp.where(first != odd, both, other)[0:1]
    down, along = iota((ROWS_DEV, LANES), 0), iota((ROWS_DEV, LANES), 1)
    wide = jnp.broadcast_to(mine, (ROWS_DEV, LANES))
    column = jnp.sum(jnp.where(down == along, wide, 0), axis=1, keepdims=True)
    earlier = (column == wide) & (down < along % ROWS_DEV)
    rank = jnp.sum(earlier.astype(jnp.int32), axis=0, keepdims=True)
    place = jnp.concatenate([mine * CAP + rank] * 4, axis=1)
    place = jnp.broadcast_to(place, (INSTS * 16, 512))
    down, along = iota((512, 512), 0), iota((512, 512), 1)
    order = (down % ROWS_DEV == along // KVH) & (down // ROWS_DEV == along % KVH)
    keyvals = dot(order.astype(jnp.float32).astype(jnp.bfloat16), keyvals_ref[...])
    keyvals = keyvals.astype(jnp.bfloat16)
    for c in range(N_TP * TILES):
        tp, tile = divmod(c, TILES)
        if tile < GROUP:
            piece = queries_ref[:, (tp * GROUP + tile) * HD : (tp * GROUP + tile + 1) * HD]
        else:
            lane = (tile - GROUP) * HD
            piece = keyvals[tp * ROWS_DEV : (tp + 1) * ROWS_DEV, lane : lane + HD]
        to, col = c % 8, c // 8
        rows_ref[to * ROWS_DEV : (to + 1) * ROWS_DEV, col * LANES : (col + 1) * LANES] = piece
    down, along = iota((INSTS * 16, 512), 0), iota((INSTS * 16, 512), 1)
    here = along // ROWS_DEV == down // 2 % 8
    wanted = down // 16 * CAP + down % 2
    size = INSTS * N_TP * MESSAGE
    copies = []
    for step in range(N_INST // INSTS):
        chosen = (place == wanted + step * INSTS * CAP) & here
        out = dot(chosen.astype(jnp.float32).astype(jnp.bfloat16), rows_ref[...])
        out = out.astype(jnp.bfloat16)
        for i in range(INSTS):
            for col in range(TILES):
                row = step * size + i * 160 + col * 16
                out_ref[row : row + 16, :] = out[
                    i * 16 : (i + 1) * 16, col * LANES : (col + 1) * LANES
                ]
        rows = pl.ds(step * size, size)
        copies.append(pltpu.make_async_copy(out_ref.at[rows], out_hbm.at[rows], sems.at[step]))
        copies[-1].start()
    for copy in copies:
        copy.wait()


def dispatch(me, targets, queries, keyvals):
    rows = N_INST * N_TP * MESSAGE
    return pl.pallas_call(
        dispatch_kernel,
        out_shape=pltpu.HBM((rows, LANES), jnp.bfloat16),
        grid_spec=pltpu.PrefetchScalarGridSpec(
            num_scalar_prefetch=1,
            grid=(1,),
            in_specs=[
                pl.BlockSpec((8, LANES), lambda s, me: (me[0] // 16, 0)),
                pl.BlockSpec((ROWS_DEV, H * HD), lambda s, me: (0, 0)),
                pl.BlockSpec((ROWS_DEV * KVH, 2 * HD), lambda s, me: (0, 0)),
            ],
            out_specs=pl.BlockSpec(memory_space=pltpu.HBM),
            scratch_shapes=[
                pltpu.VMEM((512, TILES * LANES), jnp.bfloat16),
                pltpu.VMEM((rows, LANES), jnp.bfloat16),
                pltpu.SemaphoreType.DMA((N_INST // INSTS,)),
            ],
        ),
        compiler_params=pltpu.CompilerParams(vmem_limit_bytes=VMEM),
        name="dispatch",
    )(me, *(pltpu.with_memory_space_constraint(x, pltpu.HBM) for x in (targets, queries, keyvals)))


def prepare_kernel(
    inst_ref, slot_ref, table_ref, cache_ref, target_ref, leaving_ref, context_ref, mask_ref
):
    inst = inst_ref[0]
    moved = slot_ref[inst]
    for r in range(REQ):
        for j in range(MAXP):
            page = pl.multiple_of(table_ref[r, j] * PAGE, PAGE)
            row = r * CTX + j * PAGE
            context_ref[row : row + PAGE, :] = cache_ref[pl.ds(page, PAGE), :]
    leaving_ref[...] = context_ref[pl.ds(pl.multiple_of(moved * CTX, CTX), CTX), :]
    lines = target_ref.shape[0]
    hits = (target_ref[...] == inst).astype(jnp.float32).astype(jnp.bfloat16)
    slot, along = iota((SLOTS, lines), 0), iota((SLOTS, lines), 1)
    spread = dot((slot // 4 == along).astype(jnp.float32).astype(jnp.bfloat16), hits)
    slot, along = iota((SLOTS, LANES), 0), iota((SLOTS, LANES), 1)
    spread = jnp.where(along // ROWS_DEV == slot // 2 % 2, spread, 0.0).astype(jnp.bfloat16)
    count = dot(spread, jnp.ones((LANES, LANES), jnp.bfloat16))
    mask = jnp.where(count > (slot % 2).astype(jnp.float32), 0.0, MASKED)
    mask_ref[...] = mask.astype(jnp.bfloat16)


def specs(*spaces):
    return [pl.BlockSpec(memory_space=s) for s in spaces]


def prepare(inst, slots, table, cache, targets):
    smem, vmem = pltpu.SMEM, pltpu.VMEM
    return pl.pallas_call(
        prepare_kernel,
        out_shape=(
            jax.ShapeDtypeStruct((CTX, 2 * HD), jnp.bfloat16),
            jax.ShapeDtypeStruct((REQ * CTX, 2 * HD), jnp.bfloat16),
            jax.ShapeDtypeStruct((SLOTS, LANES), jnp.bfloat16),
        ),
        in_specs=specs(smem, smem, smem, vmem, vmem),
        out_specs=specs(vmem, vmem, vmem),
        compiler_params=pltpu.CompilerParams(vmem_limit_bytes=VMEM),
        name="prepare",
    )(inst, slots, table, cache, targets)


def decode_kernel(
    inst_ref, slot_ref, lens_ref, queries_ref, fresh_ref, context_ref,
    out_ref, query_ref, newer_ref, values_ref,
):
    inst = inst_ref[0]
    rows = STEPS * REQ
    queries, fresh = queries_ref[...], fresh_ref[...]
    query = jnp.concatenate([queries[:, g * HD : (g + 1) * HD] for g in range(GROUP)], axis=0)
    n = GROUP * rows
    row = iota((n, 1), 0)
    request, moment = row % REQ, row // REQ % STEPS
    newer = dot(query, fresh[:, :HD], NT)
    along = iota((n, rows), 1)
    newer = jnp.where((along % REQ == request) & (along // REQ <= moment), newer, MASKED)
    past = jnp.zeros((n, CTX), jnp.float32)
    length = jnp.zeros((n, 1), jnp.int32)
    for r in range(REQ):
        keys = context_ref[r * CTX : (r + 1) * CTX, :HD]
        past = jnp.where(request == r, dot(query, keys, NT), past)
        length = jnp.where(request == r, lens_ref[inst * REQ + r], length)
    past = jnp.where(iota((n, CTX), 1) < length, past, MASKED)
    past, newer = shares(past, newer)
    out = dot(newer.astype(jnp.bfloat16), fresh[:, HD:])
    for r in range(REQ):
        weights = jnp.where(request == r, past, 0.0).astype(jnp.bfloat16)
        out = out + dot(weights, context_ref[r * CTX : (r + 1) * CTX, HD:])
    for g in range(GROUP):
        out_ref[:, g * HD : (g + 1) * HD] = out[g * rows : (g + 1) * rows].astype(jnp.bfloat16)

    moved = slot_ref[inst]
    chosen = iota((8, rows), 1) == iota((8, rows), 0) * REQ + moved
    picked = dot(chosen.astype(jnp.float32).astype(jnp.bfloat16), queries)
    picked = jnp.concatenate([picked[:, g * HD : (g + 1) * HD] for g in range(GROUP)], axis=0)
    picked = picked.astype(jnp.bfloat16)
    query_ref[...] = picked
    chosen = iota((LANES, rows), 1) == iota((LANES, rows), 0) * REQ + moved
    fresh = dot(chosen.astype(jnp.float32).astype(jnp.bfloat16), fresh).astype(jnp.bfloat16)
    values_ref[...] = fresh[:, HD:]
    shape = newer_ref.shape
    moment, along = iota(shape, 0) % 8, iota(shape, 1)
    newer_ref[...] = jnp.where(
        (along <= moment) & (along < STEPS), dot(picked, fresh[:, :HD], NT), MASKED
    )


def shares(past, newer):
    top = jnp.maximum(
        jnp.max(past, axis=1, keepdims=True), jnp.max(newer, axis=1, keepdims=True)
    )
    past = jnp.exp2((past - top) * LOG2_SCALE)
    newer = jnp.exp2((newer - top) * LOG2_SCALE)
    total = jnp.sum(past, axis=1, keepdims=True) + jnp.sum(newer, axis=1, keepdims=True)
    return past / total, newer / total


def decode(inst, slots, lens, queries, fresh, context):
    smem, vmem = pltpu.SMEM, pltpu.VMEM
    return pl.pallas_call(
        decode_kernel,
        out_shape=(
            jax.ShapeDtypeStruct(queries.shape, jnp.bfloat16),
            jax.ShapeDtypeStruct((GROUP * 8, HD), jnp.bfloat16),
            jax.ShapeDtypeStruct((GROUP * 8, LANES), jnp.float32),
            jax.ShapeDtypeStruct((LANES, HD), jnp.bfloat16),
        ),
        in_specs=specs(smem, smem, smem, vmem, vmem, vmem),
        out_specs=specs(vmem, vmem, vmem, vmem),
        compiler_params=pltpu.CompilerParams(vmem_limit_bytes=VMEM),
        name="decode",
    )(inst, slots, lens, queries, fresh, context)


BITS = N_INST.bit_length() - 1


def traded_kernel(
    inst_ref, partner_ref, slot_ref, lens_ref, query_ref, newer_ref, values_ref, decoded_ref, *refs
):
    *came_refs, out_ref = refs
    inst = inst_ref[0]
    other = partner_ref[inst]
    moved = slot_ref[inst]
    distance = jnp.bitwise_xor(inst, other)
    came = came_refs[0][...]
    for bit in range(1, BITS):
        came = jnp.where(distance == 1 << bit, came_refs[bit][...], came)
    past = dot(query_ref[...], came[:, :HD], NT)
    length = lens_ref[other * REQ + slot_ref[other]]
    past = jnp.where(iota(past.shape, 1) < length, past, MASKED)
    past, newer = shares(past, newer_ref[...])
    out = dot(past.astype(jnp.bfloat16), came[:, HD:])
    out = out + dot(newer.astype(jnp.bfloat16), values_ref[...])
    out = jnp.concatenate([out[g * 8 : (g + 1) * 8] for g in range(GROUP)], axis=1)
    rows, width = out_ref.shape
    out = jnp.broadcast_to(out[:STEPS, None, :], (STEPS, REQ, width)).reshape(rows, width)
    here = iota((rows, 1), 0) % REQ == moved
    out_ref[...] = jnp.where(here, out, decoded_ref[...].astype(jnp.float32)).astype(jnp.bfloat16)


def traded(inst, partner, slots, lens, query, newer, values, decoded, came):
    smem, vmem = pltpu.SMEM, pltpu.VMEM
    return pl.pallas_call(
        traded_kernel,
        out_shape=jax.ShapeDtypeStruct(decoded.shape, jnp.bfloat16),
        in_specs=specs(*[smem] * 4, *[vmem] * (4 + BITS)),
        out_specs=specs(vmem)[0],
        compiler_params=pltpu.CompilerParams(vmem_limit_bytes=VMEM),
        name="traded",
    )(inst, partner, slots, lens, query, newer, values, decoded, *came)


BLOCK = 128
HEADS = 4


def prefill_kernel(
    arrived_ref, mask_ref, out_hbm, packed_ref, keys_ref, last_ref, values_ref, out_ref, sems
):
    size = N_TP * MESSAGE
    to, src = iota((size, size), 0), iota((size, size), 1)
    order = (
        (to // 16 == src // 2 % TILES) & (to // 2 % 8 == src // MESSAGE) & (to % 2 == src % 2)
    )
    order = order.astype(jnp.float32).astype(jnp.bfloat16)
    late = iota((BLOCK, BLOCK), 0) > iota((BLOCK, BLOCK), 1)
    position = iota((BLOCK, BLOCK), 0) == iota((BLOCK, BLOCK), 1)
    position = position.astype(jnp.float32).astype(jnp.bfloat16)
    positions = jnp.concatenate([position] * HEADS, axis=0)

    def bring(start, end):
        first = start // 16
        rows = jnp.concatenate(
            [arrived_ref[(first + j) * size : (first + j + 1) * size, :] for j in range(8)], axis=1
        )
        rows = dot(order, rows).astype(jnp.bfloat16)
        for tile in range(TILES):
            for j in range(8):
                packed_ref[tile, start + j * 16 : start + (j + 1) * 16, :] = rows[
                    tile * 16 : (tile + 1) * 16, j * LANES : (j + 1) * LANES
                ]
        mask = mask_ref[start:end, :]
        keys_ref[start:end, :HD] = packed_ref[GROUP, start:end, :]
        keys_ref[start:end, HD:] = mask
        last_ref[start:end, :HD] = packed_ref[GROUP, start:end, :]
        mask = jnp.where(late, MASKED, mask.astype(jnp.float32))
        last_ref[start:end, HD:] = mask.astype(jnp.bfloat16)
        values_ref[start:end, :HD] = packed_ref[GROUP + 1, start:end, :]
        values_ref[start:end, HD:] = jnp.ones((BLOCK, LANES), jnp.bfloat16)

    def scored(start, end, heads):
        if heads[0] == 0:
            bring(start, end)
        query = jnp.concatenate([packed_ref[h, start:end, :] for h in heads], axis=0)
        query = jnp.concatenate([query, positions], axis=1)
        scores = dot(query, last_ref[start:end, :], NT)
        if start:
            scores = jnp.concatenate([dot(query, keys_ref[:start, :], NT), scores], axis=1)
        return scores

    work = [
        (start, start + BLOCK, range(h, h + HEADS))
        for start in range(0, SLOTS, BLOCK)
        for h in range(0, GROUP, HEADS)
    ]
    scores = scored(*work[0])
    copies = []
    for i, (start, end, heads) in enumerate(work):
        ahead = scored(*work[i + 1]) if i + 1 < len(work) else None
        filled = (mask_ref[start:end, 0:1].astype(jnp.float32) == 0).astype(jnp.float32)
        filled = jnp.concatenate([filled] * HEADS, axis=0)
        top = jnp.max(scores, axis=1, keepdims=True)
        expo = jnp.exp2((scores - top) * LOG2_SCALE).astype(jnp.bfloat16)
        out = dot(expo, values_ref[:end, :])
        out = (out[:, :HD] * (filled / out[:, HD:])).astype(jnp.bfloat16)
        for j, h in enumerate(heads):
            out_ref[start:end, h * HD : (h + 1) * HD] = out[j * BLOCK : (j + 1) * BLOCK]
        if heads[-1] == GROUP - 1:
            rows, sem = pl.ds(start, BLOCK), sems.at[start // BLOCK]
            copies.append(pltpu.make_async_copy(out_ref.at[rows], out_hbm.at[rows], sem))
            copies[-1].start()
        scores = ahead
    for copy in copies:
        copy.wait()


def prefill(arrived, mask):
    vmem = pltpu.VMEM
    return pl.pallas_call(
        prefill_kernel,
        out_shape=jax.ShapeDtypeStruct((SLOTS, GROUP * HD), jnp.bfloat16),
        in_specs=specs(vmem, vmem),
        out_specs=specs(pltpu.HBM)[0],
        scratch_shapes=[
            pltpu.VMEM((TILES, SLOTS, LANES), jnp.bfloat16),
            pltpu.VMEM((SLOTS, 2 * HD), jnp.bfloat16),
            pltpu.VMEM((SLOTS, 2 * HD), jnp.bfloat16),
            pltpu.VMEM((SLOTS, 2 * HD), jnp.bfloat16),
            pltpu.VMEM((SLOTS, GROUP * HD), jnp.bfloat16),
            pltpu.SemaphoreType.DMA((SLOTS // BLOCK,)),
        ],
        compiler_params=pltpu.CompilerParams(vmem_limit_bytes=VMEM),
        name="prefill",
    )(arrived, mask)


def local(
    step_queries,
    step_keyvals,
    cache_pages,
    block_table,
    context_len,
    partner,
    moved_slot,
    prompt_queries,
    prompt_keyvals,
    prompt_target,
):
    inst = lax.axis_index("inst")
    device = inst * N_TP + lax.axis_index("tp")
    targets = prompt_target.reshape(-1, LANES)
    sent = dispatch(
        device[None], targets, prompt_queries, prompt_keyvals.reshape(ROWS_DEV * KVH, 2 * HD)
    )
    arrived = lax.all_to_all(
        sent.reshape(N_INST * N_TP, MESSAGE // 4, 4, LANES), ("inst", "tp"), 0, 0, tiled=True
    ).reshape(sent.shape)

    cache = cache_pages.reshape(POOL * PAGE, 2 * HD)
    leaving, context, mask = prepare(inst[None], moved_slot, block_table, cache, targets)
    queries = step_queries.reshape(STEPS * REQ, GROUP * HD)
    fresh = step_keyvals.reshape(STEPS * REQ, 2 * HD)
    decoded, query, newer, values = decode(
        inst[None], moved_slot, context_len, queries, fresh, context
    )
    leaving, decoded = lax.optimization_barrier((leaving, decoded))
    came = [
        lax.ppermute(leaving, "inst", [(i, i ^ 1 << bit) for i in range(N_INST)])
        for bit in range(BITS)
    ]
    prefill_output = prefill(arrived, mask)
    query, prefill_output = lax.optimization_barrier((query, prefill_output))
    decoded = traded(
        inst[None], partner, moved_slot, context_len, query, newer, values, decoded, came
    )
    return decoded.reshape(step_queries.shape), prefill_output


def solution(mesh):
    placed = (
        P(None, "inst", "tp"),
        P(None, "inst", "tp", None),
        P("inst", None, "tp", None),
        P("inst", None),
        P(),
        P(),
        P(),
        P(("inst", "tp"), None),
        P(("inst", "tp"), None, None),
        P(),
    )
    return jax.shard_map(
        local,
        mesh=mesh,
        in_specs=placed,
        out_specs=(P(None, "inst", "tp"), P("inst", "tp")),
        check_vma=False,
    )
```

```python
import functools
import math

import jax
import jax.numpy as jnp
from jax import lax
from jax.experimental import pallas as pl
from jax.experimental.pallas import tpu as pltpu
from jax.sharding import PartitionSpec as P

H, KVH, HD = 64, 8, 128
REQ, PAGE, MAXP, STEPS = 8, 16, 16, 4
ROWS_DEV, CTX, POOL, CAP, SLOTS = 64, 256, 128, 2, 1024
N_INST, N_TP = 64, 8
GROUP = H // KVH
TILES = GROUP + 2
MESSAGE = TILES * CAP
LANES = 128
LOG2_SCALE = HD**-0.5 * math.log2(math.e)
MASKED = -1e30
VMEM = 48 * 1024 * 1024


def iota(shape, dim):
    return lax.broadcasted_iota(jnp.int32, shape, dim)


def dot(a, b, contract=((1,), (0,))):
    return lax.dot_general(a, b, (contract, ((), ())), preferred_element_type=jnp.float32)


NT = ((1,), (1,))


INSTS = 16


def dispatch_kernel(
    me_ref, target_ref, queries_ref, keyvals_ref, out_hbm, rows_ref, out_ref, sems
):
    me = me_ref[0]
    line = lax.rem(lax.div(me, 2), 8)
    both = jnp.sum(
        jnp.where(iota((8, LANES), 0) == line, target_ref[...], 0), axis=0, keepdims=True
    )
    both = jnp.broadcast_to(both, (8, LANES))
    other = pltpu.roll(both, ROWS_DEV, 1)
    first = iota((8, LANES), 1) < ROWS_DEV
    odd = lax.rem(me, 2) == 1
    mine = jnp.where(first != odd, both, other)[0:1]
    down, along = iota((ROWS_DEV, LANES), 0), iota((ROWS_DEV, LANES), 1)
    wide = jnp.broadcast_to(mine, (ROWS_DEV, LANES))
    column = jnp.sum(jnp.where(down == along, wide, 0), axis=1, keepdims=True)
    earlier = (column == wide) & (down < along % ROWS_DEV)
    rank = jnp.sum(earlier.astype(jnp.int32), axis=0, keepdims=True)
    place = jnp.concatenate([mine * CAP + rank] * 4, axis=1)
    place = jnp.broadcast_to(place, (INSTS * 16, 512))
    down, along = iota((512, 512), 0), iota((512, 512), 1)
    order = (down % ROWS_DEV == along // KVH) & (down // ROWS_DEV == along % KVH)
    keyvals = dot(order.astype(jnp.float32).astype(jnp.bfloat16), keyvals_ref[...])
    keyvals = keyvals.astype(jnp.bfloat16)
    for c in range(N_TP * TILES):
        tp, tile = divmod(c, TILES)
        if tile < GROUP:
            piece = queries_ref[:, (tp * GROUP + tile) * HD : (tp * GROUP + tile + 1) * HD]
        else:
            lane = (tile - GROUP) * HD
            piece = keyvals[tp * ROWS_DEV : (tp + 1) * ROWS_DEV, lane : lane + HD]
        to, col = c % 8, c // 8
        rows_ref[to * ROWS_DEV : (to + 1) * ROWS_DEV, col * LANES : (col + 1) * LANES] = piece
    down, along = iota((INSTS * 16, 512), 0), iota((INSTS * 16, 512), 1)
    here = along // ROWS_DEV == down // 2 % 8
    wanted = down // 16 * CAP + down % 2
    size = INSTS * N_TP * MESSAGE
    copies = []
    for step in range(N_INST // INSTS):
        chosen = (place == wanted + step * INSTS * CAP) & here
        out = dot(chosen.astype(jnp.float32).astype(jnp.bfloat16), rows_ref[...])
        out = out.astype(jnp.bfloat16)
        for i in range(INSTS):
            for col in range(TILES):
                row = step * size + i * 160 + col * 16
                out_ref[row : row + 16, :] = out[
                    i * 16 : (i + 1) * 16, col * LANES : (col + 1) * LANES
                ]
        rows = pl.ds(step * size, size)
        copies.append(pltpu.make_async_copy(out_ref.at[rows], out_hbm.at[rows], sems.at[step]))
        copies[-1].start()
    for copy in copies:
        copy.wait()


def dispatch(me, targets, queries, keyvals):
    rows = N_INST * N_TP * MESSAGE
    return pl.pallas_call(
        dispatch_kernel,
        out_shape=pltpu.HBM((rows, LANES), jnp.bfloat16),
        grid_spec=pltpu.PrefetchScalarGridSpec(
            num_scalar_prefetch=1,
            grid=(1,),
            in_specs=[
                pl.BlockSpec((8, LANES), lambda s, me: (me[0] // 16, 0)),
                pl.BlockSpec((ROWS_DEV, H * HD), lambda s, me: (0, 0)),
                pl.BlockSpec((ROWS_DEV * KVH, 2 * HD), lambda s, me: (0, 0)),
            ],
            out_specs=pl.BlockSpec(memory_space=pltpu.HBM),
            scratch_shapes=[
                pltpu.VMEM((512, TILES * LANES), jnp.bfloat16),
                pltpu.VMEM((rows, LANES), jnp.bfloat16),
                pltpu.SemaphoreType.DMA((N_INST // INSTS,)),
            ],
        ),
        compiler_params=pltpu.CompilerParams(vmem_limit_bytes=VMEM),
        name="dispatch",
    )(me, *(pltpu.with_memory_space_constraint(x, pltpu.HBM) for x in (targets, queries, keyvals)))


def prepare_kernel(
    inst_ref, slot_ref, table_ref, cache_ref, target_ref, leaving_ref, context_ref, mask_ref
):
    inst = inst_ref[0]
    moved = slot_ref[inst]
    for r in range(REQ):
        for j in range(MAXP):
            page = pl.multiple_of(table_ref[r, j] * PAGE, PAGE)
            row = r * CTX + j * PAGE
            context_ref[row : row + PAGE, :] = cache_ref[pl.ds(page, PAGE), :]
    leaving_ref[...] = context_ref[pl.ds(pl.multiple_of(moved * CTX, CTX), CTX), :]
    lines = target_ref.shape[0]
    hits = (target_ref[...] == inst).astype(jnp.float32).astype(jnp.bfloat16)
    slot, along = iota((SLOTS, lines), 0), iota((SLOTS, lines), 1)
    spread = dot((slot // 4 == along).astype(jnp.float32).astype(jnp.bfloat16), hits)
    slot, along = iota((SLOTS, LANES), 0), iota((SLOTS, LANES), 1)
    spread = jnp.where(along // ROWS_DEV == slot // 2 % 2, spread, 0.0).astype(jnp.bfloat16)
    count = dot(spread, jnp.ones((LANES, LANES), jnp.bfloat16))
    mask = jnp.where(count > (slot % 2).astype(jnp.float32), 0.0, MASKED)
    mask_ref[...] = mask.astype(jnp.bfloat16)


def specs(*spaces):
    return [pl.BlockSpec(memory_space=s) for s in spaces]


def prepare(inst, slots, table, cache, targets):
    smem, vmem = pltpu.SMEM, pltpu.VMEM
    return pl.pallas_call(
        prepare_kernel,
        out_shape=(
            jax.ShapeDtypeStruct((CTX, 2 * HD), jnp.bfloat16),
            jax.ShapeDtypeStruct((REQ * CTX, 2 * HD), jnp.bfloat16),
            jax.ShapeDtypeStruct((SLOTS, LANES), jnp.bfloat16),
        ),
        in_specs=specs(smem, smem, smem, vmem, vmem),
        out_specs=specs(vmem, vmem, vmem),
        compiler_params=pltpu.CompilerParams(vmem_limit_bytes=VMEM),
        name="prepare",
    )(inst, slots, table, cache, targets)


def decode_kernel(
    inst_ref, slot_ref, lens_ref, queries_ref, fresh_ref, context_ref,
    out_ref, query_ref, newer_ref, values_ref,
):
    inst = inst_ref[0]
    rows = STEPS * REQ
    queries, fresh = queries_ref[...], fresh_ref[...]
    query = jnp.concatenate([queries[:, g * HD : (g + 1) * HD] for g in range(GROUP)], axis=0)
    n = GROUP * rows
    row = iota((n, 1), 0)
    request, moment = row % REQ, row // REQ % STEPS
    newer = dot(query, fresh[:, :HD], NT)
    along = iota((n, rows), 1)
    newer = jnp.where((along % REQ == request) & (along // REQ <= moment), newer, MASKED)
    past = jnp.zeros((n, CTX), jnp.float32)
    length = jnp.zeros((n, 1), jnp.int32)
    for r in range(REQ):
        keys = context_ref[r * CTX : (r + 1) * CTX, :HD]
        past = jnp.where(request == r, dot(query, keys, NT), past)
        length = jnp.where(request == r, lens_ref[inst * REQ + r], length)
    past = jnp.where(iota((n, CTX), 1) < length, past, MASKED)
    past, newer = shares(past, newer)
    out = dot(newer.astype(jnp.bfloat16), fresh[:, HD:])
    for r in range(REQ):
        weights = jnp.where(request == r, past, 0.0).astype(jnp.bfloat16)
        out = out + dot(weights, context_ref[r * CTX : (r + 1) * CTX, HD:])
    for g in range(GROUP):
        out_ref[:, g * HD : (g + 1) * HD] = out[g * rows : (g + 1) * rows].astype(jnp.bfloat16)

    moved = slot_ref[inst]
    chosen = iota((8, rows), 1) == iota((8, rows), 0) * REQ + moved
    picked = dot(chosen.astype(jnp.float32).astype(jnp.bfloat16), queries)
    picked = jnp.concatenate([picked[:, g * HD : (g + 1) * HD] for g in range(GROUP)], axis=0)
    picked = picked.astype(jnp.bfloat16)
    query_ref[...] = picked
    chosen = iota((LANES, rows), 1) == iota((LANES, rows), 0) * REQ + moved
    fresh = dot(chosen.astype(jnp.float32).astype(jnp.bfloat16), fresh).astype(jnp.bfloat16)
    values_ref[...] = fresh[:, HD:]
    shape = newer_ref.shape
    moment, along = iota(shape, 0) % 8, iota(shape, 1)
    newer_ref[...] = jnp.where(
        (along <= moment) & (along < STEPS), dot(picked, fresh[:, :HD], NT), MASKED
    )


def shares(past, newer):
    top = jnp.maximum(
        jnp.max(past, axis=1, keepdims=True), jnp.max(newer, axis=1, keepdims=True)
    )
    past = jnp.exp2((past - top) * LOG2_SCALE)
    newer = jnp.exp2((newer - top) * LOG2_SCALE)
    total = jnp.sum(past, axis=1, keepdims=True) + jnp.sum(newer, axis=1, keepdims=True)
    return past / total, newer / total


def decode(inst, slots, lens, queries, fresh, context):
    smem, vmem = pltpu.SMEM, pltpu.VMEM
    return pl.pallas_call(
        decode_kernel,
        out_shape=(
            jax.ShapeDtypeStruct(queries.shape, jnp.bfloat16),
            jax.ShapeDtypeStruct((GROUP * 8, HD), jnp.bfloat16),
            jax.ShapeDtypeStruct((GROUP * 8, LANES), jnp.float32),
            jax.ShapeDtypeStruct((LANES, HD), jnp.bfloat16),
        ),
        in_specs=specs(smem, smem, smem, vmem, vmem, vmem),
        out_specs=specs(vmem, vmem, vmem, vmem),
        compiler_params=pltpu.CompilerParams(vmem_limit_bytes=VMEM),
        name="decode",
    )(inst, slots, lens, queries, fresh, context)


BITS = N_INST.bit_length() - 1


def traded_kernel(
    inst_ref, partner_ref, slot_ref, lens_ref, query_ref, newer_ref, values_ref, decoded_ref, *refs
):
    *came_refs, out_ref = refs
    inst = inst_ref[0]
    other = partner_ref[inst]
    moved = slot_ref[inst]
    distance = jnp.bitwise_xor(inst, other)
    came = came_refs[0][...]
    for bit in range(1, BITS):
        came = jnp.where(distance == 1 << bit, came_refs[bit][...], came)
    past = dot(query_ref[...], came[:, :HD], NT)
    length = lens_ref[other * REQ + slot_ref[other]]
    past = jnp.where(iota(past.shape, 1) < length, past, MASKED)
    past, newer = shares(past, newer_ref[...])
    out = dot(past.astype(jnp.bfloat16), came[:, HD:])
    out = out + dot(newer.astype(jnp.bfloat16), values_ref[...])
    out = jnp.concatenate([out[g * 8 : (g + 1) * 8] for g in range(GROUP)], axis=1)
    rows, width = out_ref.shape
    out = jnp.broadcast_to(out[:STEPS, None, :], (STEPS, REQ, width)).reshape(rows, width)
    here = iota((rows, 1), 0) % REQ == moved
    out_ref[...] = jnp.where(here, out, decoded_ref[...].astype(jnp.float32)).astype(jnp.bfloat16)


def traded(inst, partner, slots, lens, query, newer, values, decoded, came):
    smem, vmem = pltpu.SMEM, pltpu.VMEM
    return pl.pallas_call(
        traded_kernel,
        out_shape=jax.ShapeDtypeStruct(decoded.shape, jnp.bfloat16),
        in_specs=specs(*[smem] * 4, *[vmem] * (4 + BITS)),
        out_specs=specs(vmem)[0],
        compiler_params=pltpu.CompilerParams(vmem_limit_bytes=VMEM),
        name="traded",
    )(inst, partner, slots, lens, query, newer, values, decoded, *came)


BLOCK = 128
HEADS = 8


def prefill_kernel(
    arrived_ref, mask_ref, out_hbm, packed_ref, keys_ref, values_ref, out_ref, sems
):
    size = N_TP * MESSAGE
    to, src = iota((size, size), 0), iota((size, size), 1)
    order = (
        (to // 16 == src // 2 % TILES) & (to // 2 % 8 == src // MESSAGE) & (to % 2 == src % 2)
    )
    order = order.astype(jnp.float32).astype(jnp.bfloat16)
    late = iota((BLOCK, BLOCK), 0) > iota((BLOCK, BLOCK), 1)
    position = iota((BLOCK, BLOCK), 0) == iota((BLOCK, BLOCK), 1)
    position = position.astype(jnp.float32).astype(jnp.bfloat16)
    positions = jnp.concatenate([position] * HEADS, axis=0)

    def bring(start, end):
        first = start // 16
        rows = jnp.concatenate(
            [arrived_ref[(first + j) * size : (first + j + 1) * size, :] for j in range(8)], axis=1
        )
        rows = dot(order, rows).astype(jnp.bfloat16)
        for tile in range(TILES):
            for j in range(8):
                packed_ref[tile, start + j * 16 : start + (j + 1) * 16, :] = rows[
                    tile * 16 : (tile + 1) * 16, j * LANES : (j + 1) * LANES
                ]
        keys_ref[start:end, :HD] = packed_ref[GROUP, start:end, :]
        mask = jnp.where(late, MASKED, mask_ref[start:end, :].astype(jnp.float32))
        keys_ref[start:end, HD:] = mask.astype(jnp.bfloat16)
        if start:
            keys_ref[start - BLOCK : start, HD:] = mask_ref[start - BLOCK : start, :]
        values_ref[start:end, :HD] = packed_ref[GROUP + 1, start:end, :]
        values_ref[start:end, HD:] = jnp.ones((BLOCK, LANES), jnp.bfloat16)

    def scored(start, end, heads):
        if heads[0] == 0:
            bring(start, end)
        query = jnp.concatenate([packed_ref[h, start:end, :] for h in heads], axis=0)
        query = jnp.concatenate([query, positions], axis=1)
        return dot(query, keys_ref[:end, :], NT)

    work = [
        (start, start + BLOCK, range(h, h + HEADS))
        for start in range(0, SLOTS, BLOCK)
        for h in range(0, GROUP, HEADS)
    ]
    scores = scored(*work[0])
    copies = []
    for i, (start, end, heads) in enumerate(work):
        ahead = scored(*work[i + 1]) if i + 1 < len(work) else None
        filled = (mask_ref[start:end, 0:1].astype(jnp.float32) == 0).astype(jnp.float32)
        filled = jnp.concatenate([filled] * HEADS, axis=0)
        top = jnp.max(scores, axis=1, keepdims=True)
        expo = jnp.exp2((scores - top) * LOG2_SCALE).astype(jnp.bfloat16)
        out = dot(expo, values_ref[:end, :])
        out = (out[:, :HD] * (filled / out[:, HD:])).astype(jnp.bfloat16)
        for j, h in enumerate(heads):
            out_ref[start:end, h * HD : (h + 1) * HD] = out[j * BLOCK : (j + 1) * BLOCK]
        if heads[-1] == GROUP - 1:
            rows, sem = pl.ds(start, BLOCK), sems.at[start // BLOCK]
            copies.append(pltpu.make_async_copy(out_ref.at[rows], out_hbm.at[rows], sem))
            copies[-1].start()
        scores = ahead
    for copy in copies:
        copy.wait()


def prefill(arrived, mask):
    vmem = pltpu.VMEM
    return pl.pallas_call(
        prefill_kernel,
        out_shape=jax.ShapeDtypeStruct((SLOTS, GROUP * HD), jnp.bfloat16),
        in_specs=specs(vmem, vmem),
        out_specs=specs(pltpu.HBM)[0],
        scratch_shapes=[
            pltpu.VMEM((TILES, SLOTS, LANES), jnp.bfloat16),
            pltpu.VMEM((SLOTS, 2 * HD), jnp.bfloat16),
            pltpu.VMEM((SLOTS, 2 * HD), jnp.bfloat16),
            pltpu.VMEM((SLOTS, GROUP * HD), jnp.bfloat16),
            pltpu.SemaphoreType.DMA((SLOTS // BLOCK,)),
        ],
        compiler_params=pltpu.CompilerParams(vmem_limit_bytes=VMEM),
        name="prefill",
    )(arrived, mask)


def local(
    step_queries,
    step_keyvals,
    cache_pages,
    block_table,
    context_len,
    partner,
    moved_slot,
    prompt_queries,
    prompt_keyvals,
    prompt_target,
):
    inst = lax.axis_index("inst")
    device = inst * N_TP + lax.axis_index("tp")
    targets = prompt_target.reshape(-1, LANES)
    sent = dispatch(
        device[None], targets, prompt_queries, prompt_keyvals.reshape(ROWS_DEV * KVH, 2 * HD)
    )
    arrived = lax.all_to_all(
        sent.reshape(N_INST * N_TP, MESSAGE // 4, 4, LANES), ("inst", "tp"), 0, 0, tiled=True
    ).reshape(sent.shape)

    cache = cache_pages.reshape(POOL * PAGE, 2 * HD)
    leaving, context, mask = prepare(inst[None], moved_slot, block_table, cache, targets)
    queries = step_queries.reshape(STEPS * REQ, GROUP * HD)
    fresh = step_keyvals.reshape(STEPS * REQ, 2 * HD)
    decoded, query, newer, values = decode(
        inst[None], moved_slot, context_len, queries, fresh, context
    )
    leaving, decoded = lax.optimization_barrier((leaving, decoded))
    came = [
        lax.ppermute(leaving, "inst", [(i, i ^ 1 << bit) for i in range(N_INST)])
        for bit in range(BITS)
    ]
    prefill_output = prefill(arrived, mask)
    query, prefill_output = lax.optimization_barrier((query, prefill_output))
    decoded = traded(
        inst[None], partner, moved_slot, context_len, query, newer, values, decoded, came
    )
    return decoded.reshape(step_queries.shape), prefill_output


def solution(mesh):
    placed = (
        P(None, "inst", "tp"),
        P(None, "inst", "tp", None),
        P("inst", None, "tp", None),
        P("inst", None),
        P(),
        P(),
        P(),
        P(("inst", "tp"), None),
        P(("inst", "tp"), None, None),
        P(),
    )
    return jax.shard_map(
        local,
        mesh=mesh,
        in_specs=placed,
        out_specs=(P(None, "inst", "tp"), P("inst", "tp")),
        check_vma=False,
    )
```
